32 devices in a mesh: seq: 8 (over z, x), head: 4 (over y, core).
Axes of the slice: x: 2, y: 2, z: 4, core: 2. Of those that a mesh axis runs over, the one named last changes fastest.
Arguments:
- block_order: int32 [16], replicated, may hold values from 0 to 15, each once
- queries: bfloat16 [2048, 4096], P('seq', 'head'), may hold values from -52 to 52
- keys: bfloat16 [2048, 4096], P('seq', 'head'), may hold values from -4.5 to 4.5
- values: bfloat16 [2048, 4096], P('seq', 'head'), may hold values from -5 to 5
- hyena_q: bfloat16 [2048, 4096], P('seq', 'head'), may hold values from -5 to 5
- hyena_k: bfloat16 [2048, 4096], P('seq', 'head'), may hold values from -5 to 5
- hyena_v: bfloat16 [2048, 4096], P('seq', 'head'), may hold values from -5 to 5
- hyena_grad: bfloat16 [2048, 4096], P('seq', 'head'), may hold values from -5 to 5
- filters: float32 [256, 128], P('head'), may hold values from -0.5 to 0.5
- proj_weight: bfloat16 [3, 4096, 4096], P(None, None, 'head'), may hold values from -0.0546875 to 0.0546875
Outputs:
- input_grad: bfloat16 [2048, 4096], P('seq', 'head')
- query_grad: bfloat16 [2048, 4096], P('seq', 'head')
- key_grad: bfloat16 [2048, 4096], P('seq', 'head')
- value_grad: bfloat16 [2048, 4096], P('seq', 'head')
The draws below stay inside these ranges and needn't reach their ends.
Inputs may be any that keep to these rules, and one draw needn't show every extreme that they name: `block_order`: A permutation of the sequence blocks; entry 2 d + j is the position block of rows d * 256 + j * 128 to d * 256 + j * 128 + 127.
All inputs are finite; a program needn't handle non-finite values.
Results may differ from the reference program's by a relative error of at most 0.01.
Values may be sent and summed in bfloat16 or wider, within the bound.
A program may use at most 128 MiB of HBM per device.

```python
import jax
import jax.numpy as jnp
from jax import lax

D = 4096
HD = 128
HEADS = 32
GROUP = 16
GROUPS = 256
KL = 128
BLOCK = 128
BLOCKS = 16
TOKENS = 2048


def attention_pair(key):
    base_key = jax.random.fold_in(key, 101)
    query_key, key_key = jax.random.split(base_key, 2)
    shape = (TOKENS, HEADS, HD)
    key_rows = jnp.clip(jax.random.normal(key_key, shape, jnp.float32), -4.5, 4.5)
    query_rows = jnp.clip(jax.random.normal(query_key, shape, jnp.float32), -4.5, 4.5)
    return (query_rows.reshape(TOKENS, D), key_rows.reshape(TOKENS, D))


def draw_queries(key, part):
    return attention_pair(key)[0].astype(jnp.bfloat16)


def draw_keys(key, part):
    return attention_pair(key)[1].astype(jnp.bfloat16)


def levels(key, dims, shards, low, high):
    def one(axis_at, shards_of):
        steps = jax.random.uniform(jax.random.fold_in(jax.random.fold_in(key, 6), axis_at), (shards_of,), jnp.float32, low / len(shards), high / len(shards))
        return jnp.repeat(jnp.exp(steps), dims[axis_at] // shards_of).reshape((-1,) + (1,) * (len(dims) - axis_at - 1))

    gain = one(*shards[0])
    for cut in shards[1:]:
        gain = gain * one(*cut)
    return gain


def gaussian(rng, dims, spread, most, pieces=(), kind=jnp.bfloat16):
    entries = spread * jax.random.normal(rng, dims, jnp.float32)
    if pieces:
        entries = entries * levels(rng, dims, pieces, -0.22, 0.18)
    return jnp.clip(entries, -most, most).astype(kind)


def setup_inputs(seed: int = 0) -> dict:
    key_of = jax.random.split(jax.random.key(seed), 11)
    block_order = jax.random.permutation(key_of[0], BLOCKS).astype(jnp.int32)
    queries = draw_queries(jax.random.fold_in(key_of[10], 71), 0)
    keys = draw_keys(jax.random.fold_in(key_of[10], 71), 0)
    values = gaussian(key_of[3], (TOKENS, D), 1.0, 5.0, ((0, 8), (1, 4)))
    hyena_q = gaussian(key_of[4], (TOKENS, D), 1.0, 5.0, ((0, 8), (1, 4)))
    hyena_k = gaussian(key_of[5], (TOKENS, D), 1.0, 5.0, ((0, 8), (1, 4)))
    hyena_v = gaussian(key_of[6], (TOKENS, D), 1.0, 5.0, ((0, 8), (1, 4)))
    hyena_grad = gaussian(key_of[7], (TOKENS, D), 1.0, 5.0, ((0, 8), (1, 4)))
    filters = gaussian(key_of[8], (GROUPS, KL), KL ** -0.5, 0.5, ((0, 4),), jnp.float32)
    proj_weight = gaussian(key_of[9], (3, D, D), (3 * D) ** -0.5, 0.0546875, ((2, 4),))
    return dict(block_order=block_order, queries=queries, keys=keys, values=values, hyena_q=hyena_q, hyena_k=hyena_k, hyena_v=hyena_v, hyena_grad=hyena_grad, filters=filters, proj_weight=proj_weight)


def reference(block_order, queries, keys, values, hyena_q, hyena_k, hyena_v, hyena_grad, filters, proj_weight):
    row_ids = jnp.arange(TOKENS, dtype=jnp.int32)
    position = (block_order[row_ids // BLOCK] * BLOCK + row_ids % BLOCK).astype(jnp.int32)
    in_order = jnp.argsort(position).astype(jnp.int32)
    product_kv = (hyena_k.astype(jnp.float32) * hyena_v.astype(jnp.float32)).astype(jnp.bfloat16)
    product_dq = (hyena_grad.astype(jnp.float32) * hyena_q.astype(jnp.float32)).astype(jnp.bfloat16)
    series_z = product_kv[in_order].astype(jnp.float32)
    series_dc = product_dq[in_order].astype(jnp.float32)
    tap_table = jnp.repeat(filters, GROUP, axis=0).T
    padded_z = jnp.pad(series_z, ((KL, 0), (0, 0)))
    padded_dc = jnp.pad(series_dc, ((0, KL), (0, 0)))

    def add_tap(partial_sums, tap_index):
        conv_sum, back_sum = partial_sums
        tap_weights = lax.dynamic_index_in_dim(tap_table, tap_index, 0, keepdims=False)
        conv_sum = conv_sum + tap_weights * lax.dynamic_slice_in_dim(padded_z, KL - tap_index, TOKENS, 0)
        back_sum = back_sum + tap_weights * lax.dynamic_slice_in_dim(padded_dc, tap_index, TOKENS, 0)
        return (conv_sum, back_sum), None

    zeros_field = jnp.zeros((TOKENS, D), jnp.float32)
    scanned = lax.scan(add_tap, (zeros_field, zeros_field), jnp.arange(KL, dtype=jnp.int32))
    conv_pos, back_pos = scanned[0]
    convolved = conv_pos[position]
    back_conv = back_pos[position]
    stacked = jnp.stack([hyena_grad.astype(jnp.float32) * convolved,
                         back_conv * hyena_v.astype(jnp.float32),
                         back_conv * hyena_k.astype(jnp.float32)]).astype(jnp.bfloat16)
    summed = jnp.zeros((TOKENS, D), jnp.float32)
    for member in range(3):
        summed = summed + jnp.dot(stacked[member], proj_weight[member].T, preferred_element_type=jnp.float32)
    input_grad = summed.astype(jnp.bfloat16)

    visible = position[None, :] <= position[:, None]
    score_scale = HD ** -0.5

    def split_heads(array):
        return array.reshape(TOKENS, HEADS, HD).transpose(1, 0, 2)

    def head_grads(operands):
        query_h, key_h, value_h, output_grad = operands
        scores = jnp.dot(query_h, key_h.T, preferred_element_type=jnp.float32) * score_scale
        scores = jnp.where(visible, scores, -1e30)
        row_top = jnp.max(scores, axis=1, keepdims=True)
        exponent_terms = jnp.where(visible, jnp.exp(scores - row_top), 0.0)
        probabilities = exponent_terms / jnp.sum(exponent_terms, axis=1, keepdims=True)
        prob_grad = jnp.dot(output_grad, value_h.T, preferred_element_type=jnp.float32)
        row_delta = jnp.sum(probabilities * prob_grad, axis=1, keepdims=True)
        score_grad = probabilities * (prob_grad - row_delta)
        probs_low = probabilities.astype(jnp.bfloat16)
        score_low = score_grad.astype(jnp.bfloat16)
        grad_query = (jnp.dot(score_low, key_h, preferred_element_type=jnp.float32) * score_scale).astype(jnp.bfloat16)
        grad_key = (jnp.dot(score_low.T, query_h, preferred_element_type=jnp.float32) * score_scale).astype(jnp.bfloat16)
        grad_value = jnp.dot(probs_low.T, output_grad, preferred_element_type=jnp.float32).astype(jnp.bfloat16)
        return grad_query, grad_key, grad_value

    head_results = lax.map(head_grads, (split_heads(queries), split_heads(keys), split_heads(values), split_heads(input_grad)))

    def join_heads(array):
        return array.transpose(1, 0, 2).reshape(TOKENS, D)

    return input_grad, join_heads(head_results[0]), join_heads(head_results[1]), join_heads(head_results[2])
```

```python
import functools

import jax
import jax.numpy as jnp
from jax import lax
from jax.experimental import pallas as pl
from jax.experimental.pallas import tpu as pltpu
from jax.sharding import PartitionSpec as P

HD = 128
GROUP = 16
KL = 128
BLOCK = 128


def for_sending(x):

    def short(part):
        return part.astype(jnp.bfloat16) if part.dtype == jnp.float32 else part

    return jax.tree.map(short, x)


def passed_along(value, axis, steps):
    count = lax.axis_size(axis)
    pairs = [(source, (source + steps) % count) for source in range(count)]
    return lax.ppermute(value, axis, pairs)


def keep_state(current):
    return current


def ring_device(
    block_order, queries, keys, values, hyena_q, hyena_k, hyena_v, hyena_grad, filters, proj_weight
):
    seq_count = lax.axis_size("seq")
    my_index = lax.axis_index("seq")
    row_count = queries.shape[0]
    feature_width = queries.shape[1]
    head_count = feature_width // HD
    block_total = block_order.shape[0]
    offsets = jnp.arange(BLOCK, dtype=jnp.int32)
    block_ids = jnp.arange(block_total, dtype=jnp.int32)

    def block_positions(source):
        block_pair = lax.dynamic_slice_in_dim(block_order, 2 * source, 2)
        return jnp.concatenate([block_pair[0] * BLOCK + offsets, block_pair[1] * BLOCK + offsets])

    def holder_of(target):
        return jnp.sum(jnp.where(block_order == target, block_ids, 0))

    my_positions = block_positions(my_index)
    product_kv = (hyena_k.astype(jnp.float32) * hyena_v.astype(jnp.float32)).astype(jnp.bfloat16)
    product_dq = (hyena_grad.astype(jnp.float32) * hyena_q.astype(jnp.float32)).astype(jnp.bfloat16)
    my_blocks = [
        lax.dynamic_index_in_dim(block_order, 2 * my_index + portion, 0, keepdims=False)
        for portion in range(2)
    ]
    gathered_z, gathered_dc = (
        lax.all_gather(product_kv, "seq", axis=0, tiled=True),
        lax.all_gather(product_dq, "seq", axis=0, tiled=True),
    )
    group_count = filters.shape[0]
    channels = hyena_q.shape[1]
    out_rows = jnp.arange(BLOCK)[:, None, None]
    window_rows = jnp.arange(BLOCK + KL)[None, :, None]
    tap_ids = jnp.arange(KL)[None, None, :]
    causal_table = (out_rows + KL - window_rows == tap_ids).astype(jnp.float32)
    anti_table = (window_rows - out_rows == tap_ids).astype(jnp.float32)
    causal_toeplitz = jnp.einsum(
        "gj,tsj->gts", filters, causal_table, precision=lax.Precision.HIGHEST
    )
    anti_toeplitz = jnp.einsum("gj,tsj->gts", filters, anti_table, precision=lax.Precision.HIGHEST)

    def apply_groups(toeplitz, window):
        grouped = window.astype(jnp.float32).reshape(BLOCK + KL, group_count, GROUP)
        result = jnp.einsum("gts,sgk->tgk", toeplitz, grouped, precision=lax.Precision.HIGHEST)
        return result.reshape(BLOCK, channels)

    conv_parts = []
    back_parts = []
    for portion in range(2):
        block_id = my_blocks[portion]
        before = lax.dynamic_slice_in_dim(
            gathered_z, holder_of(block_id - 1) * BLOCK + BLOCK - KL, KL, 0
        )
        before = jnp.where(block_id >= 1, before, jnp.zeros_like(before))
        after = lax.dynamic_slice_in_dim(gathered_dc, holder_of(block_id + 1) * BLOCK, KL, 0)
        after = jnp.where(block_id + 1 < block_total, after, jnp.zeros_like(after))
        own_z = product_kv[portion * BLOCK : (portion + 1) * BLOCK]
        own_dc = product_dq[portion * BLOCK : (portion + 1) * BLOCK]
        conv_parts.append(apply_groups(causal_toeplitz, jnp.concatenate([before, own_z])))
        back_parts.append(apply_groups(anti_toeplitz, jnp.concatenate([own_dc, after])))
    convolved = jnp.concatenate(conv_parts)
    back_conv = jnp.concatenate(back_parts)
    stacked = jnp.stack(
        [
            hyena_grad.astype(jnp.float32) * convolved,
            back_conv * hyena_v.astype(jnp.float32),
            back_conv * hyena_k.astype(jnp.float32),
        ]
    ).astype(jnp.bfloat16)
    summed = lax.psum_scatter(
        jnp.einsum("mic,mtc->it", proj_weight, stacked, preferred_element_type=jnp.float32),
        "head",
        scatter_dimension=0,
        tiled=True,
    )
    input_grad = summed.T.astype(jnp.bfloat16)
    score_scale = HD ** (-0.5)
    query_heads = queries.reshape(row_count, head_count, HD)
    key_heads = keys.reshape(row_count, head_count, HD)
    value_heads = values.reshape(row_count, head_count, HD)
    grad_heads = input_grad.reshape(row_count, head_count, HD)

    def tile_scores(query_block, key_block, query_pos, key_pos):
        scores = (
            jnp.einsum("qhd,khd->hqk", query_block, key_block, preferred_element_type=jnp.float32)
            * score_scale
        )
        allowed = (key_pos[None, :] <= query_pos[:, None])[None]
        return (scores, allowed)

    def stat_update(running, key_block, value_block, source):
        key_pos = block_positions(source)
        active = jnp.min(key_pos) <= jnp.max(my_positions)

        def stat_accumulate(current):
            row_max, row_sum, row_dot = current
            scores, allowed = tile_scores(query_heads, key_block, my_positions, key_pos)
            masked = jnp.where(allowed, scores, -1e30)
            new_max = jnp.maximum(row_max, jnp.max(masked, axis=2))
            terms = jnp.where(allowed, jnp.exp(masked - new_max[:, :, None]), 0.0)
            prob_grad = jnp.einsum(
                "qhd,khd->hqk", grad_heads, value_block, preferred_element_type=jnp.float32
            )
            factor = jnp.exp(row_max - new_max)
            return (
                new_max,
                row_sum * factor + jnp.sum(terms, axis=2),
                row_dot * factor + jnp.sum(terms * prob_grad, axis=2),
            )

        return lax.cond(active, stat_accumulate, keep_state, running)

    initial = (
        jnp.full((head_count, row_count), -1e30, jnp.float32),
        jnp.zeros((head_count, row_count), jnp.float32),
        jnp.zeros((head_count, row_count), jnp.float32),
    )

    def tile_grads(
        query_block, grad_block, norm_block, delta_block, query_pos, key_block, value_block, key_pos
    ):
        scores, allowed = tile_scores(query_block, key_block, query_pos, key_pos)
        probabilities = jnp.where(allowed, jnp.exp(scores - norm_block[:, :, None]), 0.0)
        prob_grad = jnp.einsum(
            "qhd,khd->hqk", grad_block, value_block, preferred_element_type=jnp.float32
        )
        score_grad = probabilities * (prob_grad - delta_block[:, :, None])
        probs_low = probabilities.astype(jnp.bfloat16)
        score_low = score_grad.astype(jnp.bfloat16)
        add_query = (
            jnp.einsum("hqk,khd->qhd", score_low, key_block, preferred_element_type=jnp.float32)
            * score_scale
        )
        add_key = (
            jnp.einsum("hqk,qhd->khd", score_low, query_block, preferred_element_type=jnp.float32)
            * score_scale
        )
        add_value = jnp.einsum(
            "hqk,qhd->khd", probs_low, grad_block, preferred_element_type=jnp.float32
        )
        return (add_query, add_key, add_value)

    zero_rows = jnp.zeros((row_count, head_count, HD), jnp.float32)

    def move_stat_queries(pair):
        return jax.tree.map(
            lambda part, own: part.astype(own.dtype),
            passed_along(for_sending(pair), "seq", 1),
            pair,
        )

    def stat_turn(turn_index, loop_state):
        running, key_block, value_block = loop_state
        source = (my_index - turn_index) % seq_count
        running = stat_update(running, key_block, value_block, source)
        key_block, value_block = move_stat_queries((key_block, value_block))
        return (running, key_block, value_block)

    loop_state = lax.fori_loop(0, seq_count - 1, stat_turn, (initial, key_heads, value_heads))
    running = stat_update(
        loop_state[0], loop_state[1], loop_state[2], (my_index - (seq_count - 1)) % seq_count
    )
    log_norm = running[0] + jnp.log(running[1])
    row_delta = running[2] / running[1]

    def query_turn(turn_index, loop_state):
        query_block, grad_block, norm_block, delta_block, query_acc, key_acc, value_acc = loop_state
        source = (my_index - turn_index) % seq_count
        query_pos = block_positions(source)
        active = jnp.min(my_positions) <= jnp.max(query_pos)

        def query_accumulate(current):
            add_query, add_key, add_value = tile_grads(
                query_block,
                grad_block,
                norm_block,
                delta_block,
                query_pos,
                key_heads,
                value_heads,
                my_positions,
            )
            return (current[0] + add_query, current[1] + add_key, current[2] + add_value)

        query_acc, key_acc, value_acc = lax.cond(
            active, query_accumulate, keep_state, (query_acc, key_acc, value_acc)
        )
        query_block, grad_block = passed_along((query_block, grad_block), "seq", 1)
        norm_block, delta_block, query_acc = passed_along(
            (norm_block, delta_block, query_acc), "seq", 1
        )
        return (query_block, grad_block, norm_block, delta_block, query_acc, key_acc, value_acc)

    final_state = lax.fori_loop(
        0,
        seq_count,
        query_turn,
        (query_heads, grad_heads, log_norm, row_delta, zero_rows, zero_rows, zero_rows),
    )
    query_total = final_state[4]
    key_total = final_state[5]
    value_total = final_state[6]
    query_grad = query_total.reshape(row_count, feature_width).astype(jnp.bfloat16)
    key_grad = key_total.reshape(row_count, feature_width).astype(jnp.bfloat16)
    value_grad = value_total.reshape(row_count, feature_width).astype(jnp.bfloat16)
    return (input_grad, query_grad, key_grad, value_grad)


MESH = pl.DeviceIdType.MESH
VMEM_SPEC = pl.BlockSpec(memory_space=pltpu.VMEM)
ANY_SPEC = pl.BlockSpec(memory_space=pl.ANY)
SMEM_SPEC = pl.BlockSpec(memory_space=pltpu.SMEM)


def aligned(index, size):
    return pl.ds(pl.multiple_of(index * size, size), size)


def fused_kernel(
    n, heads, slots,
    order_ref, filters_ref, hq_in, hk_in, hv_in, hg_in, q_in, k_in, v_in, weight_in,
    grad_ref, dq_ref, dk_ref, dv_ref,
    hq, hk, hv, hg, qs, ks, vs, z_own, dc_own,
    zc, dcc, z_out, dc_out, z_far, dc_far,
    causal, anti, convc, dzc, conv, dz, stacked, weights,
    total, pair_in, line_out, line_in,
    qc, kc, vc, gc, keys, keys_t, values, prob, dq_sum, dk_sum, dv_sum, dq_low, dk_low, dv_low,
    holder, after, before, z_cross, dc_cross, z_rank, dc_rank, z_pick, dc_pick,
    load_sem, weight_sem, own_sem, send_sem, recv_sem,
    half_send, half_recv, half_own, far_send, far_recv, pair_sem, line_sem,
):
    me = lax.axis_index("seq")
    head = lax.axis_index("head")
    chips = heads // 2
    chip, core = head // 2, lax.rem(head, 2)
    partner = chip * 2 + 1 - core
    along = [lax.rem(chip + step, chips) for step in range(chips)]
    steps = list(range(1, chips)) + [0]
    blocks = order_ref.shape[0]
    members = n // 2
    held = blocks // 2
    side, place = me // members, lax.rem(me, members)
    base = side * held
    width = hq.shape[2]
    part = zc.shape[2]
    groups = part // GROUP
    tile = 2 * BLOCK
    tiles = width // tile

    loads = [
        pltpu.make_async_copy(source, target, load_sem.at[i])
        for i, (source, target) in enumerate(
            ((hg_in, hg), (hq_in, hq), (hk_in, hk), (hv_in, hv), (q_in, qs), (k_in, ks), (v_in, vs))
        )
    ]
    for copy in loads:
        copy.start()

    def weight_copy(m, slot):
        return pltpu.make_async_copy(weight_in.at[m], weights.at[slot], weight_sem.at[m])

    weight_copy(1, 0).start()
    weight_copy(2, 1).start()

    barrier = pltpu.get_barrier_semaphore()
    for step in range(1, n):
        pl.semaphore_signal(
            barrier, inc=1, device_id={"seq": lax.rem(me + step, n)}, device_id_type=MESH
        )
    head_peers = [partner] + [along[step] * 2 + core for step in range(1, chips)]
    for peer in head_peers:
        pl.semaphore_signal(barrier, inc=1, device_id={"head": peer}, device_id_type=MESH)

    def wide_of(ref):
        return ref[...].astype(jnp.float32)

    loads[0].wait()
    loads[1].wait()
    dc_own[...] = (wide_of(hg) * wide_of(hq)).astype(jnp.bfloat16)
    loads[2].wait()
    loads[3].wait()
    z_own[...] = (wide_of(hk) * wide_of(hv)).astype(jnp.bfloat16)
    pl.semaphore_wait(barrier, n - 1 + len(head_peers))

    def to_head(tensor, src, dst, step):
        peer = lax.rem(me + step, n)
        return pltpu.make_async_remote_copy(
            src_ref=src.at[:, :, aligned(peer, HD)], dst_ref=dst.at[aligned(me, 2)],
            send_sem=send_sem.at[tensor, step], recv_sem=recv_sem.at[tensor, step],
            device_id={"seq": peer}, device_id_type=MESH,
        )

    def to_rows(tensor, src, dst, step):
        peer = lax.rem(me + step, n)
        return pltpu.make_async_remote_copy(
            src_ref=src.at[aligned(peer, 2)], dst_ref=dst.at[:, :, aligned(me, HD)],
            send_sem=send_sem.at[tensor, step], recv_sem=recv_sem.at[tensor, step],
            device_id={"seq": peer}, device_id_type=MESH,
        )

    def own_head(tensor, src, dst):
        return pltpu.make_async_copy(
            src.at[:, :, aligned(me, HD)], dst.at[aligned(me, 2)], own_sem.at[tensor]
        )

    def own_rows(tensor, src, dst):
        return pltpu.make_async_copy(
            src.at[aligned(me, 2)], dst.at[:, :, aligned(me, HD)], own_sem.at[tensor]
        )

    def start_all(make, own, tensor, src, dst):
        for step in range(1, n):
            make(tensor, src, dst, step).start()
        own(tensor, src, dst).start()

    def wait_all(make, own, tensor, src, dst):
        for step in range(1, n):
            make(tensor, src, dst, step).wait()
        own(tensor, src, dst).wait()

    def spread(tensor, src, dst, step):
        goal = lax.rem(place + step, members)
        return pltpu.make_async_remote_copy(
            src_ref=src.at[:, :, aligned(goal, part)], dst_ref=dst.at[aligned(place, 2)],
            send_sem=half_send.at[tensor, step], recv_sem=half_recv.at[tensor, step],
            device_id={"seq": side * members + goal}, device_id_type=MESH,
        )

    def spread_own(tensor, src, dst):
        return pltpu.make_async_copy(
            src.at[:, :, aligned(place, part)], dst.at[aligned(place, 2)], half_own.at[tensor]
        )

    def collect(tensor, src, dst, step):
        goal = lax.rem(place + step, members)
        return pltpu.make_async_remote_copy(
            src_ref=src.at[aligned(goal, 2)], dst_ref=dst.at[:, :, aligned(place, part)],
            send_sem=half_send.at[tensor, step], recv_sem=half_recv.at[tensor, step],
            device_id={"seq": side * members + goal}, device_id_type=MESH,
        )

    def collect_own(tensor, src, dst):
        return pltpu.make_async_copy(
            src.at[aligned(place, 2)], dst.at[:, :, aligned(place, part)], half_own.at[tensor]
        )

    def cross(tensor, src, dst):
        return pltpu.make_async_remote_copy(
            src_ref=src, dst_ref=dst.at[pl.ds(0, slots)],
            send_sem=far_send.at[tensor], recv_sem=far_recv.at[tensor],
            device_id={"seq": lax.rem(me + members, n)}, device_id_type=MESH,
        )

    for tensor, src, dst in ((0, dc_own, dcc), (1, z_own, zc)):
        for step in range(1, members):
            spread(tensor, src, dst, step).start()
        spread_own(tensor, src, dst).start()

    order = [order_ref[r] for r in range(blocks)]
    for p in range(blocks):
        found = jnp.int32(0)
        for r in range(1, blocks):
            found = jnp.where(order[r] == p, r, found)
        holder[p] = found
    for start in (0, held):
        z_count, dc_count = jnp.int32(0), jnp.int32(0)
        for r in range(start, start + held):
            later = holder[jnp.minimum(order[r] + 1, blocks - 1)]
            later = jnp.where(order[r] + 1 < blocks, later, r)
            sooner = holder[jnp.maximum(order[r] - 1, 0)]
            sooner = jnp.where(order[r] > 0, sooner, r)
            leaves = (later < held) if start else (later >= held)
            returns = (sooner < held) if start else (sooner >= held)
            leaves = jnp.where(leaves, 1, 0)
            returns = jnp.where(returns, 1, 0)
            after[r], before[r] = later, sooner
            z_cross[r], dc_cross[r] = leaves, returns
            z_rank[r], dc_rank[r] = z_count, dc_count
            z_count, dc_count = z_count + leaves, dc_count + returns
    for pick, crossing, rank in ((dc_pick, dc_cross, dc_rank), (z_pick, z_cross, z_rank)):
        flags = [crossing[base + l] for l in range(held)]
        ranks = [rank[base + l] for l in range(held)]
        for k in range(slots):
            found = jnp.int32(0)
            for l in range(1, held):
                found = jnp.where((flags[l] == 1) & (ranks[l] == k), l, found)
            pick[k] = found

    window = 2 * BLOCK
    taps = filters_ref[aligned(place, groups), :]
    flip = jnp.where(
        lax.broadcasted_iota(jnp.int32, (KL, KL), 0) + lax.broadcasted_iota(jnp.int32, (KL, KL), 1)
        == KL - 1, 1.0, 0.0,
    ).astype(jnp.bfloat16)
    high = taps.astype(jnp.bfloat16)
    low = (taps - high.astype(jnp.float32)).astype(jnp.bfloat16)
    turned = jnp.dot(high, flip, preferred_element_type=jnp.float32)
    turned = turned + jnp.dot(low, flip, preferred_element_type=jnp.float32)
    for table, rows, shift in ((anti, taps, 0), (causal, turned, 1)):
        padded = jnp.concatenate([rows, jnp.zeros_like(rows)], axis=1)
        for g in range(groups):
            line = jnp.broadcast_to(padded[g : g + 1, :], (BLOCK, window))
            line = pltpu.roll(line, shift, 1, stride=1, stride_axis=0)
            top = line.astype(jnp.bfloat16)
            table[:BLOCK, g * window : (g + 1) * window] = top
            table[BLOCK:, g * window : (g + 1) * window] = (
                line - top.astype(jnp.float32)
            ).astype(jnp.bfloat16)

    for tensor, src, dst, pick, out, far in (
        (0, dc_own, dcc, dc_pick, dc_out, dc_far), (1, z_own, zc, z_pick, z_out, z_far)
    ):
        for step in range(1, members):
            spread(tensor, src, dst, step).wait()
        spread_own(tensor, src, dst).wait()
        for k in range(slots):
            out[k] = dst[pick[k]]
        cross(tensor, out, far).start()

    lane_group = lax.broadcasted_iota(jnp.int32, (window, window), 1) % HD // GROUP
    chunks = part // HD
    chunk_groups = groups // chunks

    def filtered(goal, near, far, linked, end, rank, table, target, own_first):
        pairs = []
        for half in range(2):
            local = goal * 2 + half
            row = base + local
            own = near[local]
            link = linked[row]
            inside = (link >= base) & (link < base + held)
            some = jnp.where(order_ref[row] == end, 0.0, 1.0)
            here = jnp.where(inside, some, 0.0)
            there = jnp.where(inside, 0.0, some)
            found = near[jnp.where(inside, link - base, 0)].astype(jnp.float32) * here
            sent = far[jnp.where(inside, 0, jnp.minimum(rank[link], slots - 1))]
            other = (found + sent.astype(jnp.float32) * there).astype(jnp.bfloat16)
            pairs.append((own, other) if own_first else (other, own))
        for c in range(chunks):
            lanes = slice(c * HD, (c + 1) * HD)
            wide = jnp.concatenate(
                [jnp.concatenate([a[:, lanes], b[:, lanes]], axis=0) for a, b in pairs], axis=1
            )
            stack = jnp.concatenate(
                [
                    jnp.where(lane_group == g, wide, jnp.zeros_like(wide))
                    for g in range(chunk_groups)
                ],
                axis=0,
            )
            span = chunk_groups * window
            result = jnp.dot(
                table[:, c * span : (c + 1) * span], stack, preferred_element_type=jnp.float32
            )
            result = (result[:BLOCK] + result[BLOCK:]).astype(target.dtype)
            target[goal * 2, :, lanes] = result[:, :HD]
            target[goal * 2 + 1, :, lanes] = result[:, HD:]

    def send_back(tensor, near, far, linked, end, rank, table, target, out, own_first):
        def one(step, carry):
            goal = lax.rem(place + step, members)
            filtered(goal, near, far, linked, end, rank, table, target, own_first)
            collect(tensor, target, out, step).start()
            return carry

        lax.fori_loop(1, members, one, 0)
        filtered(place, near, far, linked, end, rank, table, target, own_first)
        collect_own(tensor, target, out).start()

    def returned(tensor, target, out):
        for step in range(1, members):
            collect(tensor, target, out, step).wait()
        collect_own(tensor, target, out).wait()

    def rows_of(value):
        return value.reshape(tile, width)

    cross(0, dc_out, dc_far).wait()
    send_back(2, dcc, dc_far, after, blocks - 1, dc_rank, anti, dzc, dz, True)
    cross(1, z_out, z_far).wait()
    send_back(3, zc, z_far, before, 0, z_rank, causal, convc, conv, False)
    attention = ((0, qs, qc), (1, ks, kc), (2, vs, vc))
    for t, src, dst in attention:
        loads[4 + t].wait()
        start_all(to_head, own_head, t, src, dst)

    goals = []
    for step in steps:
        goals.append(along[step] * 2 + 1 - core)
        goals.append(along[step] * 2 + core)

    def product(m, slot, goal, j):
        return lax.dot_general(
            stacked[m], weights[slot, aligned(goal * tiles + j, tile), :],
            (((1,), (1,)), ((), ())), preferred_element_type=jnp.float32,
        )

    returned(2, dzc, dz)
    wide = wide_of(dz)
    stacked[1] = rows_of((wide * wide_of(hv)).astype(jnp.bfloat16))
    stacked[2] = rows_of((wide * wide_of(hk)).astype(jnp.bfloat16))
    weight_copy(1, 0).wait()
    weight_copy(2, 1).wait()
    for slot, goal in enumerate(goals):
        def begin(j, carry, slot=slot, goal=goal):
            total[slot, j] = product(1, 0, goal, j) + product(2, 1, goal, j)
            return carry

        lax.fori_loop(0, tiles, begin, 0)
    weight_copy(0, 0).start()
    returned(3, convc, conv)
    stacked[0] = rows_of((wide_of(hg) * wide_of(conv)).astype(jnp.bfloat16))
    weight_copy(0, 0).wait()

    def pair_copy(at, j):
        return pltpu.make_async_remote_copy(
            src_ref=total.at[2 * at, j], dst_ref=pair_in.at[at, j],
            send_sem=pair_sem.at[0, at, j], recv_sem=pair_sem.at[1, at, j],
            device_id={"head": partner}, device_id_type=MESH,
        )

    def line_copy(at, j):
        return pltpu.make_async_remote_copy(
            src_ref=line_out.at[at, j], dst_ref=line_in.at[at, j],
            send_sem=line_sem.at[0, at, j], recv_sem=line_sem.at[1, at, j],
            device_id={"head": along[steps[at]] * 2 + core}, device_id_type=MESH,
        )

    for at in range(chips):
        def give_pair(j, carry, at=at):
            total[2 * at, j] += product(0, 0, goals[2 * at], j)
            pair_copy(at, j).start()
            return carry

        lax.fori_loop(0, tiles, give_pair, 0)

        def keep(j, carry, at=at):
            value = total[2 * at + 1, j] + product(0, 0, goals[2 * at + 1], j)
            if at < chips - 1:
                pair_copy(at, j).wait()
                line_out[at, j] = (value + pair_in[at, j]).astype(line_out.dtype)
                line_copy(at, j).start()
            else:
                total[2 * at + 1, j] = value
            return carry

        lax.fori_loop(0, tiles, keep, 0)
    last = chips - 1
    for j in range(tiles):
        pair_copy(last, j).wait()
        value = total[2 * last + 1, j] + pair_in[last, j]
        for at in range(last):
            line_copy(at, j).wait()
            value = value + line_in[at, j].astype(jnp.float32)
        grad_ref[:, :, j * tile : (j + 1) * tile] = value.astype(grad_ref.dtype).reshape(
            2, BLOCK, tile
        )
    start_all(to_head, own_head, 3, grad_ref, gc)

    scale = HD ** (-0.5)
    contract_last = (((1,), (1,)), ((), ()))
    wait_all(to_head, own_head, *attention[0])
    wait_all(to_head, own_head, *attention[1])
    for b in range(blocks):
        here = slice(b * BLOCK, (b + 1) * BLOCK)
        rows = kc[holder[b]]
        keys[here, :] = rows
        keys_t[:, here] = rows.T

    def pair(ref, i):
        return jnp.concatenate([ref[holder[2 * i]], ref[holder[2 * i + 1]]], axis=0)

    def add(sums, value, i):
        value = value.reshape(2 * i + 2, BLOCK, HD)
        if i == blocks // 2 - 1:
            sums[...] = value
        else:
            sums[: 2 * i + 2] += value

    def stored(i):
        return slice(tile * i * (i + 1) // 2, tile * (i + 1) * (i + 2) // 2)

    def give(sums, factor, low):
        for s in range(blocks):
            rows = sums[order_ref[s]]
            rows = rows if factor is None else rows * factor
            low[s] = rows.astype(low.dtype)

    for i in reversed(range(blocks // 2)):
        depth = (i + 1) * tile
        scores = lax.dot_general(
            keys[:depth, :], pair(qc, i), contract_last, preferred_element_type=jnp.float32
        ) * scale
        key_at = lax.broadcasted_iota(jnp.int32, (tile, tile), 0)
        query_at = lax.broadcasted_iota(jnp.int32, (tile, tile), 1)
        edge = jnp.where(key_at <= query_at, scores[depth - tile :], -1e30)
        scores = jnp.concatenate([scores[: depth - tile], edge], axis=0) if i else edge
        terms = jnp.exp(scores - jnp.max(scores, axis=0, keepdims=True))
        prob[stored(i), :] = terms * (1.0 / jnp.sum(terms, axis=0, keepdims=True))

    wait_all(to_head, own_head, 3, grad_ref, gc)
    for i in reversed(range(blocks // 2)):
        chance = prob[stored(i), :].astype(jnp.bfloat16)
        add(dv_sum, jnp.dot(chance, pair(gc, i), preferred_element_type=jnp.float32), i)
    give(dv_sum, None, dv_low)
    start_all(to_rows, own_rows, 4, dv_low, dv_ref)
    wait_all(to_head, own_head, *attention[2])
    for b in range(blocks):
        values[b * BLOCK : (b + 1) * BLOCK, :] = vc[holder[b]]
    for i in reversed(range(blocks // 2)):
        depth = (i + 1) * tile
        prob_grad = lax.dot_general(
            values[:depth, :], pair(gc, i), contract_last, preferred_element_type=jnp.float32
        )
        chance = prob[stored(i), :]
        delta = jnp.sum(chance * prob_grad, axis=0, keepdims=True)
        score_grad = (chance * (prob_grad - delta)).astype(jnp.bfloat16)
        add(dk_sum, jnp.dot(score_grad, pair(qc, i), preferred_element_type=jnp.float32), i)
        query_t = jnp.dot(keys_t[:, :depth], score_grad, preferred_element_type=jnp.float32)
        dq_sum[2 * i : 2 * i + 2] = (query_t.T * scale).reshape(2, BLOCK, HD)
    give(dq_sum, None, dq_low)
    start_all(to_rows, own_rows, 5, dq_low, dq_ref)
    give(dk_sum, scale, dk_low)
    start_all(to_rows, own_rows, 6, dk_low, dk_ref)
    wait_all(to_rows, own_rows, 4, dv_low, dv_ref)
    wait_all(to_rows, own_rows, 5, dq_low, dq_ref)
    wait_all(to_rows, own_rows, 6, dk_low, dk_ref)


def fused(n, heads, slots, collective, order, filters, *tensors):
    rows, width = tensors[0].shape
    weight = tensors[-1]
    blocks = order.shape[0]
    held = blocks // 2
    chips = heads // 2
    part = width // (n // 2)
    groups = part // GROUP
    tile = 2 * BLOCK
    tiles = width // tile
    stored = tile * (blocks // 2) * (blocks // 2 + 1) // 2
    bf16 = jnp.bfloat16
    local = pltpu.VMEM((2, BLOCK, width), bf16)
    mine = pltpu.VMEM((held, BLOCK, part), bf16)
    few = pltpu.VMEM((slots, BLOCK, part), bf16)
    table = pltpu.VMEM((2 * BLOCK, groups * 2 * BLOCK), bf16)
    column = pltpu.VMEM((blocks, BLOCK, HD), bf16)
    sums = pltpu.VMEM((blocks, BLOCK, HD), jnp.float32)
    dma = pltpu.SemaphoreType.DMA
    like = jax.ShapeDtypeStruct((2, BLOCK, width), bf16)
    return pl.pallas_call(
        functools.partial(fused_kernel, n, heads, slots),
        out_shape=[like] * 4,
        in_specs=[SMEM_SPEC, VMEM_SPEC] + [ANY_SPEC] * 8,
        out_specs=[VMEM_SPEC] * 4,
        scratch_shapes=[local] * 9
        + [mine] * 2
        + [few] * 4
        + [table] * 2
        + [mine] * 2
        + [local] * 2
        + [pltpu.VMEM((3, rows, width), bf16), pltpu.VMEM((2,) + weight.shape[1:], bf16)]
        + [
            pltpu.VMEM((2 * chips, tiles, rows, tile), jnp.float32),
            pltpu.VMEM((chips, tiles, rows, tile), jnp.float32),
            pltpu.VMEM((chips - 1, tiles, rows, tile), bf16),
            pltpu.VMEM((chips - 1, tiles, rows, tile), bf16),
        ]
        + [column] * 4
        + [
            pltpu.VMEM((blocks * BLOCK, HD), bf16),
            pltpu.VMEM((HD, blocks * BLOCK), bf16),
            pltpu.VMEM((blocks * BLOCK, HD), bf16),
            pltpu.VMEM((stored, tile), jnp.float32),
        ]
        + [sums] * 3
        + [column] * 3
        + [pltpu.SMEM((blocks,), jnp.int32)] * 7
        + [pltpu.SMEM((slots,), jnp.int32)] * 2
        + [
            dma((7,)), dma((3,)), dma((7,)), dma((7, n)), dma((7, n)),
            dma((4, n // 2)), dma((4, n // 2)), dma((4,)), dma((2,)), dma((2,)),
            dma((2, chips, tiles)), dma((2, chips, tiles)),
        ],
        compiler_params=pltpu.CompilerParams(
            collective_id=collective, has_side_effects=True, vmem_limit_bytes=61 * 2**20
        ),
    )(order, filters, *[t.reshape(2, BLOCK, width) for t in tensors[:-1]], weight)


def land_kernel(count, *refs):
    copies = [
        pltpu.make_async_copy(source, target, refs[-1].at[i])
        for i, (source, target) in enumerate(zip(refs[:count], refs[count:-1]))
    ]
    for copy in copies:
        copy.start()
    for copy in copies:
        copy.wait()


def land(*arrays):
    count = len(arrays)
    return pl.pallas_call(
        functools.partial(land_kernel, count),
        out_shape=[jax.ShapeDtypeStruct(a.shape, a.dtype) for a in arrays],
        in_specs=[VMEM_SPEC] * count,
        out_specs=[ANY_SPEC] * count,
        scratch_shapes=[pltpu.SemaphoreType.DMA((count,))],
        compiler_params=pltpu.CompilerParams(vmem_limit_bytes=2**20),
    )(*arrays)


def column_device(
    block_order, queries, keys, values, hyena_q, hyena_k, hyena_v, hyena_grad, filters, proj_weight
):
    n = lax.axis_size("seq")
    heads = lax.axis_size("head")
    held = block_order.shape[0] // 2
    grads = fused(
        n, heads, held, 0, block_order, filters,
        hyena_q, hyena_k, hyena_v, hyena_grad, queries, keys, values, proj_weight,
    )
    return tuple(out.reshape(queries.shape) for out in land(*grads))


def per_device(*arrays):
    queries, filters = arrays[1], arrays[8]
    n = lax.axis_size("seq")
    whole_heads = queries.shape[1] == n * HD and queries.shape[0] == 2 * BLOCK
    paired = lax.axis_size("head") % 2 == 0 and lax.axis_size("head") > 2
    split = n % 4 == 0 and filters.shape[0] % (8 * n) == 0
    if whole_heads and paired and split and KL == BLOCK == HD:
        return column_device(*arrays)
    return ring_device(*arrays)


def solution(mesh):
    placed = (
        P(),
        P("seq", "head"),
        P("seq", "head"),
        P("seq", "head"),
        P("seq", "head"),
        P("seq", "head"),
        P("seq", "head"),
        P("seq", "head"),
        P("head", None),
        P(None, None, "head"),
    )
    return jax.shard_map(
        per_device,
        mesh=mesh,
        in_specs=placed,
        out_specs=(P("seq", "head"), P("seq", "head"), P("seq", "head"), P("seq", "head")),
        check_vma=False,
    )
```

```python
import functools

import jax
import jax.numpy as jnp
from jax import lax
from jax.experimental import pallas as pl
from jax.experimental.pallas import tpu as pltpu
from jax.sharding import PartitionSpec as P

HD = 128
GROUP = 16
KL = 128
BLOCK = 128


def for_sending(x):

    def short(part):
        return part.astype(jnp.bfloat16) if part.dtype == jnp.float32 else part

    return jax.tree.map(short, x)


def passed_along(value, axis, steps):
    count = lax.axis_size(axis)
    pairs = [(source, (source + steps) % count) for source in range(count)]
    return lax.ppermute(value, axis, pairs)


def keep_state(current):
    return current


def ring_device(
    block_order, queries, keys, values, hyena_q, hyena_k, hyena_v, hyena_grad, filters, proj_weight
):
    seq_count = lax.axis_size("seq")
    my_index = lax.axis_index("seq")
    row_count = queries.shape[0]
    feature_width = queries.shape[1]
    head_count = feature_width // HD
    block_total = block_order.shape[0]
    offsets = jnp.arange(BLOCK, dtype=jnp.int32)
    block_ids = jnp.arange(block_total, dtype=jnp.int32)

    def block_positions(source):
        block_pair = lax.dynamic_slice_in_dim(block_order, 2 * source, 2)
        return jnp.concatenate([block_pair[0] * BLOCK + offsets, block_pair[1] * BLOCK + offsets])

    def holder_of(target):
        return jnp.sum(jnp.where(block_order == target, block_ids, 0))

    my_positions = block_positions(my_index)
    product_kv = (hyena_k.astype(jnp.float32) * hyena_v.astype(jnp.float32)).astype(jnp.bfloat16)
    product_dq = (hyena_grad.astype(jnp.float32) * hyena_q.astype(jnp.float32)).astype(jnp.bfloat16)
    my_blocks = [
        lax.dynamic_index_in_dim(block_order, 2 * my_index + portion, 0, keepdims=False)
        for portion in range(2)
    ]
    gathered_z, gathered_dc = (
        lax.all_gather(product_kv, "seq", axis=0, tiled=True),
        lax.all_gather(product_dq, "seq", axis=0, tiled=True),
    )
    group_count = filters.shape[0]
    channels = hyena_q.shape[1]
    out_rows = jnp.arange(BLOCK)[:, None, None]
    window_rows = jnp.arange(BLOCK + KL)[None, :, None]
    tap_ids = jnp.arange(KL)[None, None, :]
    causal_table = (out_rows + KL - window_rows == tap_ids).astype(jnp.float32)
    anti_table = (window_rows - out_rows == tap_ids).astype(jnp.float32)
    causal_toeplitz = jnp.einsum(
        "gj,tsj->gts", filters, causal_table, precision=lax.Precision.HIGHEST
    )
    anti_toeplitz = jnp.einsum("gj,tsj->gts", filters, anti_table, precision=lax.Precision.HIGHEST)

    def apply_groups(toeplitz, window):
        grouped = window.astype(jnp.float32).reshape(BLOCK + KL, group_count, GROUP)
        result = jnp.einsum("gts,sgk->tgk", toeplitz, grouped, precision=lax.Precision.HIGHEST)
        return result.reshape(BLOCK, channels)

    conv_parts = []
    back_parts = []
    for portion in range(2):
        block_id = my_blocks[portion]
        before = lax.dynamic_slice_in_dim(
            gathered_z, holder_of(block_id - 1) * BLOCK + BLOCK - KL, KL, 0
        )
        before = jnp.where(block_id >= 1, before, jnp.zeros_like(before))
        after = lax.dynamic_slice_in_dim(gathered_dc, holder_of(block_id + 1) * BLOCK, KL, 0)
        after = jnp.where(block_id + 1 < block_total, after, jnp.zeros_like(after))
        own_z = product_kv[portion * BLOCK : (portion + 1) * BLOCK]
        own_dc = product_dq[portion * BLOCK : (portion + 1) * BLOCK]
        conv_parts.append(apply_groups(causal_toeplitz, jnp.concatenate([before, own_z])))
        back_parts.append(apply_groups(anti_toeplitz, jnp.concatenate([own_dc, after])))
    convolved = jnp.concatenate(conv_parts)
    back_conv = jnp.concatenate(back_parts)
    stacked = jnp.stack(
        [
            hyena_grad.astype(jnp.float32) * convolved,
            back_conv * hyena_v.astype(jnp.float32),
            back_conv * hyena_k.astype(jnp.float32),
        ]
    ).astype(jnp.bfloat16)
    summed = lax.psum_scatter(
        jnp.einsum("mic,mtc->it", proj_weight, stacked, preferred_element_type=jnp.float32),
        "head",
        scatter_dimension=0,
        tiled=True,
    )
    input_grad = summed.T.astype(jnp.bfloat16)
    score_scale = HD ** (-0.5)
    query_heads = queries.reshape(row_count, head_count, HD)
    key_heads = keys.reshape(row_count, head_count, HD)
    value_heads = values.reshape(row_count, head_count, HD)
    grad_heads = input_grad.reshape(row_count, head_count, HD)

    def tile_scores(query_block, key_block, query_pos, key_pos):
        scores = (
            jnp.einsum("qhd,khd->hqk", query_block, key_block, preferred_element_type=jnp.float32)
            * score_scale
        )
        allowed = (key_pos[None, :] <= query_pos[:, None])[None]
        return (scores, allowed)

    def stat_update(running, key_block, value_block, source):
        key_pos = block_positions(source)
        active = jnp.min(key_pos) <= jnp.max(my_positions)

        def stat_accumulate(current):
            row_max, row_sum, row_dot = current
            scores, allowed = tile_scores(query_heads, key_block, my_positions, key_pos)
            masked = jnp.where(allowed, scores, -1e30)
            new_max = jnp.maximum(row_max, jnp.max(masked, axis=2))
            terms = jnp.where(allowed, jnp.exp(masked - new_max[:, :, None]), 0.0)
            prob_grad = jnp.einsum(
                "qhd,khd->hqk", grad_heads, value_block, preferred_element_type=jnp.float32
            )
            factor = jnp.exp(row_max - new_max)
            return (
                new_max,
                row_sum * factor + jnp.sum(terms, axis=2),
                row_dot * factor + jnp.sum(terms * prob_grad, axis=2),
            )

        return lax.cond(active, stat_accumulate, keep_state, running)

    initial = (
        jnp.full((head_count, row_count), -1e30, jnp.float32),
        jnp.zeros((head_count, row_count), jnp.float32),
        jnp.zeros((head_count, row_count), jnp.float32),
    )

    def tile_grads(
        query_block, grad_block, norm_block, delta_block, query_pos, key_block, value_block, key_pos
    ):
        scores, allowed = tile_scores(query_block, key_block, query_pos, key_pos)
        probabilities = jnp.where(allowed, jnp.exp(scores - norm_block[:, :, None]), 0.0)
        prob_grad = jnp.einsum(
            "qhd,khd->hqk", grad_block, value_block, preferred_element_type=jnp.float32
        )
        score_grad = probabilities * (prob_grad - delta_block[:, :, None])
        probs_low = probabilities.astype(jnp.bfloat16)
        score_low = score_grad.astype(jnp.bfloat16)
        add_query = (
            jnp.einsum("hqk,khd->qhd", score_low, key_block, preferred_element_type=jnp.float32)
            * score_scale
        )
        add_key = (
            jnp.einsum("hqk,qhd->khd", score_low, query_block, preferred_element_type=jnp.float32)
            * score_scale
        )
        add_value = jnp.einsum(
            "hqk,qhd->khd", probs_low, grad_block, preferred_element_type=jnp.float32
        )
        return (add_query, add_key, add_value)

    zero_rows = jnp.zeros((row_count, head_count, HD), jnp.float32)

    def move_stat_queries(pair):
        return jax.tree.map(
            lambda part, own: part.astype(own.dtype),
            passed_along(for_sending(pair), "seq", 1),
            pair,
        )

    def stat_turn(turn_index, loop_state):
        running, key_block, value_block = loop_state
        source = (my_index - turn_index) % seq_count
        running = stat_update(running, key_block, value_block, source)
        key_block, value_block = move_stat_queries((key_block, value_block))
        return (running, key_block, value_block)

    loop_state = lax.fori_loop(0, seq_count - 1, stat_turn, (initial, key_heads, value_heads))
    running = stat_update(
        loop_state[0], loop_state[1], loop_state[2], (my_index - (seq_count - 1)) % seq_count
    )
    log_norm = running[0] + jnp.log(running[1])
    row_delta = running[2] / running[1]

    def query_turn(turn_index, loop_state):
        query_block, grad_block, norm_block, delta_block, query_acc, key_acc, value_acc = loop_state
        source = (my_index - turn_index) % seq_count
        query_pos = block_positions(source)
        active = jnp.min(my_positions) <= jnp.max(query_pos)

        def query_accumulate(current):
            add_query, add_key, add_value = tile_grads(
                query_block,
                grad_block,
                norm_block,
                delta_block,
                query_pos,
                key_heads,
                value_heads,
                my_positions,
            )
            return (current[0] + add_query, current[1] + add_key, current[2] + add_value)

        query_acc, key_acc, value_acc = lax.cond(
            active, query_accumulate, keep_state, (query_acc, key_acc, value_acc)
        )
        query_block, grad_block = passed_along((query_block, grad_block), "seq", 1)
        norm_block, delta_block, query_acc = passed_along(
            (norm_block, delta_block, query_acc), "seq", 1
        )
        return (query_block, grad_block, norm_block, delta_block, query_acc, key_acc, value_acc)

    final_state = lax.fori_loop(
        0,
        seq_count,
        query_turn,
        (query_heads, grad_heads, log_norm, row_delta, zero_rows, zero_rows, zero_rows),
    )
    query_total = final_state[4]
    key_total = final_state[5]
    value_total = final_state[6]
    query_grad = query_total.reshape(row_count, feature_width).astype(jnp.bfloat16)
    key_grad = key_total.reshape(row_count, feature_width).astype(jnp.bfloat16)
    value_grad = value_total.reshape(row_count, feature_width).astype(jnp.bfloat16)
    return (input_grad, query_grad, key_grad, value_grad)


MESH = pl.DeviceIdType.MESH
VMEM_SPEC = pl.BlockSpec(memory_space=pltpu.VMEM)
ANY_SPEC = pl.BlockSpec(memory_space=pl.ANY)
SMEM_SPEC = pl.BlockSpec(memory_space=pltpu.SMEM)


LOG2E = 1.4426950408889634


def aligned(index, size):
    return pl.ds(pl.multiple_of(index * size, size), size)


def fused_kernel(
    n, heads, slots,
    order_ref, filters_ref, hq_in, hk_in, hv_in, hg_in, q_in, k_in, v_in, weight_in,
    grad_out, dq_ref, dk_ref, dv_ref,
    hq, hk, hv, hg, qs, ks, vs, z_own, dc_own, grad_ref,
    zc, dcc, z_out, dc_out, z_far, dc_far,
    lines, causal, anti, convc, dzc, conv, dz, stacked, weights,
    total, pair_in, line_out, line_in,
    qc, kc, vc, gc, keys, keys_t, values, prob, inverse, dq_sum, dk_sum, dv_sum, dq_low, dk_low, dv_low,
    holder, after, before, z_cross, dc_cross, z_rank, dc_rank, z_pick, dc_pick,
    load_sem, weight_sem, last_sem, own_sem, send_sem, recv_sem,
    half_send, half_recv, half_own, far_send, far_recv, pair_sem, line_sem,
):
    me = lax.axis_index("seq")
    head = lax.axis_index("head")
    chips = heads // 2
    chip, core = head // 2, lax.rem(head, 2)
    partner = chip * 2 + 1 - core
    along = [lax.rem(chip + step, chips) for step in range(chips)]
    steps = list(range(1, chips)) + [0]
    blocks = order_ref.shape[0]
    members = n // 2
    held = blocks // 2
    side, place = me // members, lax.rem(me, members)
    base = side * held
    width = hq.shape[2]
    part = zc.shape[2]
    groups = part // GROUP
    tile = 2 * BLOCK
    tiles = width // tile

    loads = [
        pltpu.make_async_copy(source, target, load_sem.at[i])
        for i, (source, target) in enumerate(
            ((hg_in, hg), (hq_in, hq), (hk_in, hk), (hv_in, hv), (q_in, qs), (k_in, ks), (v_in, vs))
        )
    ]
    for copy in loads:
        copy.start()

    def weight_copy(m, slot):
        return pltpu.make_async_copy(weight_in.at[m], weights.at[slot], weight_sem.at[m])

    barrier = pltpu.get_barrier_semaphore()
    for step in range(1, n):
        pl.semaphore_signal(
            barrier, inc=1, device_id={"seq": lax.rem(me + step, n)}, device_id_type=MESH
        )
    head_peers = [partner] + [along[step] * 2 + core for step in range(1, chips)]
    for peer in head_peers:
        pl.semaphore_signal(barrier, inc=1, device_id={"head": peer}, device_id_type=MESH)

    def wide_of(ref):
        return ref[...].astype(jnp.float32)

    loads[0].wait()
    loads[1].wait()
    dc_own[...] = (wide_of(hg) * wide_of(hq)).astype(jnp.bfloat16)
    loads[2].wait()
    loads[3].wait()
    z_own[...] = (wide_of(hk) * wide_of(hv)).astype(jnp.bfloat16)
    weight_copy(1, 0).start()
    weight_copy(2, 1).start()
    pl.semaphore_wait(barrier, n - 1 + len(head_peers))

    far_steps, near_steps = list(range(members)), list(range(members + 1, n))
    mixed = [s for both in zip(far_steps, near_steps) for s in both] + far_steps[len(near_steps) :]

    def peer_at(step):
        if step < members:
            return (1 - side) * members + lax.rem(place + step, members)
        return side * members + lax.rem(place + step - members, members)

    def to_head(tensor, src, dst, step):
        peer = peer_at(step)
        return pltpu.make_async_remote_copy(
            src_ref=src.at[:, :, aligned(peer, HD)], dst_ref=dst.at[aligned(me, 2)],
            send_sem=send_sem.at[tensor, step], recv_sem=recv_sem.at[tensor, step],
            device_id={"seq": peer}, device_id_type=MESH,
        )

    def to_rows(tensor, src, dst, step):
        peer = peer_at(step)
        return pltpu.make_async_remote_copy(
            src_ref=src.at[aligned(peer, 2)], dst_ref=dst.at[:, :, aligned(me, HD)],
            send_sem=send_sem.at[tensor, step], recv_sem=recv_sem.at[tensor, step],
            device_id={"seq": peer}, device_id_type=MESH,
        )

    def own_head(tensor, src, dst):
        return pltpu.make_async_copy(
            src.at[:, :, aligned(me, HD)], dst.at[aligned(me, 2)], own_sem.at[tensor]
        )

    def own_rows(tensor, src, dst):
        return pltpu.make_async_copy(
            src.at[aligned(me, 2)], dst.at[:, :, aligned(me, HD)], own_sem.at[tensor]
        )

    def start_all(make, own, tensor, src, dst):
        for step in mixed:
            make(tensor, src, dst, step).start()
        own(tensor, src, dst).start()

    def wait_all(make, own, tensor, src, dst):
        for step in mixed:
            make(tensor, src, dst, step).wait()
        own(tensor, src, dst).wait()

    def spread(tensor, src, dst, step):
        goal = lax.rem(place + step, members)
        return pltpu.make_async_remote_copy(
            src_ref=src.at[:, :, aligned(goal, part)], dst_ref=dst.at[aligned(place, 2)],
            send_sem=half_send.at[tensor, step], recv_sem=half_recv.at[tensor, step],
            device_id={"seq": side * members + goal}, device_id_type=MESH,
        )

    def spread_own(tensor, src, dst):
        return pltpu.make_async_copy(
            src.at[:, :, aligned(place, part)], dst.at[aligned(place, 2)], half_own.at[tensor]
        )

    def collect(tensor, src, dst, step):
        goal = lax.rem(place + step, members)
        return pltpu.make_async_remote_copy(
            src_ref=src.at[aligned(goal, 2)], dst_ref=dst.at[:, :, aligned(place, part)],
            send_sem=half_send.at[tensor, step], recv_sem=half_recv.at[tensor, step],
            device_id={"seq": side * members + goal}, device_id_type=MESH,
        )

    def collect_own(tensor, src, dst):
        return pltpu.make_async_copy(
            src.at[aligned(place, 2)], dst.at[:, :, aligned(place, part)], half_own.at[tensor]
        )

    def cross(tensor, src, dst):
        return pltpu.make_async_remote_copy(
            src_ref=src, dst_ref=dst.at[pl.ds(0, slots)],
            send_sem=far_send.at[tensor], recv_sem=far_recv.at[tensor],
            device_id={"seq": lax.rem(me + members, n)}, device_id_type=MESH,
        )

    for tensor, src, dst in ((0, dc_own, dcc), (1, z_own, zc)):
        for step in range(1, members):
            spread(tensor, src, dst, step).start()
        spread_own(tensor, src, dst).start()
    loads[4].wait()
    loads[5].wait()
    inner = place // (members // 2) != side

    @pl.when(inner)
    def _():
        for step in far_steps:
            to_head(0, qs, qc, step).start()

    order = [order_ref[r] for r in range(blocks)]
    for p in range(blocks):
        found = jnp.int32(0)
        for r in range(1, blocks):
            found = jnp.where(order[r] == p, r, found)
        holder[p] = found
    for start in (0, held):
        z_count, dc_count = jnp.int32(0), jnp.int32(0)
        for r in range(start, start + held):
            later = holder[jnp.minimum(order[r] + 1, blocks - 1)]
            later = jnp.where(order[r] + 1 < blocks, later, r)
            sooner = holder[jnp.maximum(order[r] - 1, 0)]
            sooner = jnp.where(order[r] > 0, sooner, r)
            leaves = (later < held) if start else (later >= held)
            returns = (sooner < held) if start else (sooner >= held)
            leaves = jnp.where(leaves, 1, 0)
            returns = jnp.where(returns, 1, 0)
            after[r], before[r] = later, sooner
            z_cross[r], dc_cross[r] = leaves, returns
            z_rank[r], dc_rank[r] = z_count, dc_count
            z_count, dc_count = z_count + leaves, dc_count + returns
    for pick, crossing, rank in ((dc_pick, dc_cross, dc_rank), (z_pick, z_cross, z_rank)):
        flags = [crossing[base + l] for l in range(held)]
        ranks = [rank[base + l] for l in range(held)]
        for k in range(slots):
            found = jnp.int32(0)
            for l in range(1, held):
                found = jnp.where((flags[l] == 1) & (ranks[l] == k), l, found)
            pick[k] = found

    for tensor, src, dst, pick, out, far in (
        (0, dc_own, dcc, dc_pick, dc_out, dc_far), (1, z_own, zc, z_pick, z_out, z_far)
    ):
        for step in range(1, members):
            spread(tensor, src, dst, step).wait()
        spread_own(tensor, src, dst).wait()
        for k in range(slots):
            out[k] = dst[pick[k]]
        cross(tensor, out, far).start()
    window = 2 * BLOCK
    taps = filters_ref[aligned(place, groups), :]
    flip = jnp.where(
        lax.broadcasted_iota(jnp.int32, (KL, KL), 0) + lax.broadcasted_iota(jnp.int32, (KL, KL), 1)
        == KL - 1, 1.0, 0.0,
    ).astype(jnp.bfloat16)
    high = taps.astype(jnp.bfloat16)
    low = (taps - high.astype(jnp.float32)).astype(jnp.bfloat16)
    turned = jnp.dot(high, flip, preferred_element_type=jnp.float32)
    turned = turned + jnp.dot(low, flip, preferred_element_type=jnp.float32)
    for at, rows in ((0, taps), (1, turned)):
        lines[at] = jnp.concatenate([rows, jnp.zeros_like(rows)], axis=1)

    def build(g, carry):
        lanes = aligned(g, window)
        for at, table in ((0, anti), (1, causal)):
            line = jnp.broadcast_to(lines[at, pl.ds(g, 1), :], (BLOCK, window))
            line = pltpu.roll(line, at, 1, stride=1, stride_axis=0)
            top = line.astype(jnp.bfloat16)
            table[:BLOCK, lanes] = top
            table[BLOCK:, lanes] = (line - top.astype(jnp.float32)).astype(jnp.bfloat16)
        return carry

    lax.fori_loop(0, groups, build, 0)

    lane_group = lax.broadcasted_iota(jnp.int32, (window, window), 1) % HD // GROUP
    chunks = part // HD
    chunk_groups = groups // chunks

    def filtered(goal, near, far, linked, end, rank, table, target, own_first):
        pairs = []
        for half in range(2):
            local = goal * 2 + half
            row = base + local
            own = near[local]
            link = linked[row]
            inside = (link >= base) & (link < base + held)
            some = jnp.where(order_ref[row] == end, 0.0, 1.0)
            here = jnp.where(inside, some, 0.0)
            there = jnp.where(inside, 0.0, some)
            found = near[jnp.where(inside, link - base, 0)].astype(jnp.float32) * here
            sent = far[jnp.where(inside, 0, jnp.minimum(rank[link], slots - 1))]
            other = (found + sent.astype(jnp.float32) * there).astype(jnp.bfloat16)
            pairs.append((own, other) if own_first else (other, own))
        for c in range(chunks):
            lanes = slice(c * HD, (c + 1) * HD)
            wide = jnp.concatenate(
                [jnp.concatenate([a[:, lanes], b[:, lanes]], axis=0) for a, b in pairs], axis=1
            )
            stack = jnp.concatenate(
                [
                    jnp.where(lane_group == g, wide, jnp.zeros_like(wide))
                    for g in range(chunk_groups)
                ],
                axis=0,
            )
            span = chunk_groups * window
            result = jnp.dot(
                table[:, c * span : (c + 1) * span], stack, preferred_element_type=jnp.float32
            )
            result = (result[:BLOCK] + result[BLOCK:]).astype(target.dtype)
            target[goal * 2, :, lanes] = result[:, :HD]
            target[goal * 2 + 1, :, lanes] = result[:, HD:]

    def send_back(tensor, near, far, linked, end, rank, table, target, out, own_first):
        def one(step, carry):
            goal = lax.rem(place + step, members)
            filtered(goal, near, far, linked, end, rank, table, target, own_first)

            @pl.when(step < members)
            def _():
                collect(tensor, target, out, step).start()

            return carry

        lax.fori_loop(1, members + 1, one, 0)
        collect_own(tensor, target, out).start()

    def returned(tensor, target, out):
        for step in range(1, members):
            collect(tensor, target, out, step).wait()
        collect_own(tensor, target, out).wait()

    def rows_of(value):
        return value.reshape(tile, width)

    cross(0, dc_out, dc_far).wait()
    send_back(2, dcc, dc_far, after, blocks - 1, dc_rank, anti, dzc, dz, True)
    cross(1, z_out, z_far).wait()

    @pl.when(inner)
    def _():
        for step in far_steps:
            to_head(1, ks, kc, step).start()

    send_back(3, zc, z_far, before, 0, z_rank, causal, convc, conv, False)
    attention = ((0, qs, qc), (1, ks, kc), (2, vs, vc))

    @pl.when(jnp.logical_not(inner))
    def _():
        for step in far_steps:
            to_head(0, qs, qc, step).start()
        for step in far_steps:
            to_head(1, ks, kc, step).start()

    for step in near_steps:
        to_head(0, qs, qc, step).start()
    own_head(0, qs, qc).start()
    for step in near_steps:
        to_head(1, ks, kc, step).start()
    own_head(1, ks, kc).start()
    loads[6].wait()
    start_all(to_head, own_head, *attention[2])

    goals = []
    for step in steps:
        goals.append(along[step] * 2 + 1 - core)
        goals.append(along[step] * 2 + core)

    def last_weight(slot):
        rows = aligned(goals[slot], width)
        return pltpu.make_async_copy(
            weight_in.at[0, rows], weights.at[0, rows], last_sem.at[slot]
        )

    def product(m, slot, goal, j):
        return lax.dot_general(
            stacked[m], weights[slot, aligned(goal * tiles + j, tile), :],
            (((1,), (1,)), ((), ())), preferred_element_type=jnp.float32,
        )

    returned(2, dzc, dz)
    wide = wide_of(dz)
    stacked[1] = rows_of((wide * wide_of(hv)).astype(jnp.bfloat16))
    stacked[2] = rows_of((wide * wide_of(hk)).astype(jnp.bfloat16))
    weight_copy(1, 0).wait()
    weight_copy(2, 1).wait()
    for slot, goal in enumerate(goals):
        def begin(j, carry, slot=slot, goal=goal):
            total[slot, j] = product(1, 0, goal, j) + product(2, 1, goal, j)
            return carry

        lax.fori_loop(0, tiles, begin, 0)
        last_weight(slot).start()
    returned(3, convc, conv)
    stacked[0] = rows_of((wide_of(hg) * wide_of(conv)).astype(jnp.bfloat16))

    def pair_copy(at, j):
        return pltpu.make_async_remote_copy(
            src_ref=total.at[2 * at, j], dst_ref=pair_in.at[at, j],
            send_sem=pair_sem.at[0, at, j], recv_sem=pair_sem.at[1, at, j],
            device_id={"head": partner}, device_id_type=MESH,
        )

    def line_copy(at, j):
        return pltpu.make_async_remote_copy(
            src_ref=line_out.at[at, j], dst_ref=line_in.at[at, j],
            send_sem=line_sem.at[0, at, j], recv_sem=line_sem.at[1, at, j],
            device_id={"head": along[steps[at]] * 2 + core}, device_id_type=MESH,
        )

    for at in range(chips):
        last_weight(2 * at).wait()

        def give_pair(j, carry, at=at):
            total[2 * at, j] += product(0, 0, goals[2 * at], j)
            pair_copy(at, j).start()
            return carry

        lax.fori_loop(0, tiles, give_pair, 0)
        last_weight(2 * at + 1).wait()

        def keep(j, carry, at=at):
            value = total[2 * at + 1, j] + product(0, 0, goals[2 * at + 1], j)
            if at < chips - 1:
                pair_copy(at, j).wait()
                line_out[at, j] = (value + pair_in[at, j]).astype(line_out.dtype)
                line_copy(at, j).start()
            else:
                total[2 * at + 1, j] = value
            return carry

        lax.fori_loop(0, tiles, keep, 0)
    last = chips - 1
    for j in range(tiles):
        pair_copy(last, j).wait()
        value = total[2 * last + 1, j] + pair_in[last, j]
        for at in range(last):
            line_copy(at, j).wait()
            value = value + line_in[at, j].astype(jnp.float32)
        grad_ref[:, :, j * tile : (j + 1) * tile] = value.astype(grad_ref.dtype).reshape(
            2, BLOCK, tile
        )
    start_all(to_head, own_head, 3, grad_ref, gc)
    grad_copy = pltpu.make_async_copy(grad_ref, grad_out, load_sem.at[7])
    grad_copy.start()

    scale = HD ** (-0.5)
    contract_last = (((1,), (1,)), ((), ()))
    wait_all(to_head, own_head, *attention[0])
    wait_all(to_head, own_head, *attention[1])
    for b in range(blocks):
        here = slice(b * BLOCK, (b + 1) * BLOCK)
        rows = kc[holder[b]]
        keys[here, :] = rows
        keys_t[:, here] = rows.T

    def pair(ref, i):
        return jnp.concatenate([ref[holder[2 * i]], ref[holder[2 * i + 1]]], axis=0)

    def add(sums, value, i):
        value = value.reshape(2 * i + 2, BLOCK, HD)
        if i == blocks // 2 - 1:
            sums[...] = value
        else:
            sums[: 2 * i + 2] += value

    def chance_of(i):
        first = i * (i + 1) // 2
        terms = prob[first : first + i + 1].reshape((i + 1) * tile, tile)
        return terms * inverse[i]

    def give(sums, factor, low):
        for s in range(blocks):
            rows = sums[order_ref[s]]
            rows = rows if factor is None else rows * factor
            low[s] = rows.astype(low.dtype)

    key_at = lax.broadcasted_iota(jnp.int32, (tile, tile), 0)
    query_at = lax.broadcasted_iota(jnp.int32, (tile, tile), 1)
    rate = scale * LOG2E

    def folded(value, op):
        value = value.reshape(tile // 8, 8, tile)
        return op(value, axis=0)

    def chances(i, carry):
        q = pair(qc, i)
        first = i * (i + 1) // 2

        def score(j, top):
            value = lax.dot_general(
                keys[aligned(j, tile), :], q, contract_last, preferred_element_type=jnp.float32
            )
            prob[first + j] = value
            return jnp.maximum(top, folded(value, jnp.max))

        top = lax.fori_loop(0, i, score, jnp.full((8, tile), -1e30, jnp.float32))
        value = lax.dot_general(
            keys[aligned(i, tile), :], q, contract_last, preferred_element_type=jnp.float32
        )
        value = jnp.where(key_at <= query_at, value, -1e30)
        prob[first + i] = value
        top = jnp.maximum(top, folded(value, jnp.max))
        top = jnp.max(top, axis=0, keepdims=True)

        def term(j, sums):
            value = jnp.exp2((prob[first + j] - top) * rate)
            prob[first + j] = value
            return sums + folded(value, jnp.sum)

        sums = lax.fori_loop(0, i + 1, term, jnp.zeros((8, tile), jnp.float32))
        inverse[i] = 1.0 / jnp.sum(sums, axis=0, keepdims=True)
        return carry

    lax.fori_loop(0, blocks // 2, chances, 0)

    wait_all(to_head, own_head, 3, grad_ref, gc)
    for i in reversed(range(blocks // 2)):
        chance = chance_of(i).astype(jnp.bfloat16)
        add(dv_sum, jnp.dot(chance, pair(gc, i), preferred_element_type=jnp.float32), i)
    give(dv_sum, None, dv_low)
    start_all(to_rows, own_rows, 4, dv_low, dv_ref)
    wait_all(to_head, own_head, *attention[2])
    for b in range(blocks):
        values[b * BLOCK : (b + 1) * BLOCK, :] = vc[holder[b]]
    for i in reversed(range(blocks // 2)):
        depth = (i + 1) * tile
        prob_grad = lax.dot_general(
            values[:depth, :], pair(gc, i), contract_last, preferred_element_type=jnp.float32
        )
        chance = chance_of(i)
        delta = jnp.sum(chance * prob_grad, axis=0, keepdims=True)
        score_grad = (chance * (prob_grad - delta)).astype(jnp.bfloat16)
        add(dk_sum, jnp.dot(score_grad, pair(qc, i), preferred_element_type=jnp.float32), i)
        query_t = jnp.dot(keys_t[:, :depth], score_grad, preferred_element_type=jnp.float32)
        dq_sum[2 * i : 2 * i + 2] = (query_t.T * scale).reshape(2, BLOCK, HD)
    give(dq_sum, None, dq_low)
    start_all(to_rows, own_rows, 5, dq_low, dq_ref)
    give(dk_sum, scale, dk_low)
    start_all(to_rows, own_rows, 6, dk_low, dk_ref)
    grad_copy.wait()
    wait_all(to_rows, own_rows, 4, dv_low, dv_ref)
    wait_all(to_rows, own_rows, 5, dq_low, dq_ref)
    wait_all(to_rows, own_rows, 6, dk_low, dk_ref)


def fused(n, heads, slots, collective, order, filters, *tensors):
    rows, width = tensors[0].shape
    weight = tensors[-1]
    blocks = order.shape[0]
    held = blocks // 2
    chips = heads // 2
    part = width // (n // 2)
    groups = part // GROUP
    tile = 2 * BLOCK
    tiles = width // tile
    stored = (blocks // 2) * (blocks // 2 + 1) // 2
    bf16 = jnp.bfloat16
    local = pltpu.VMEM((2, BLOCK, width), bf16)
    mine = pltpu.VMEM((held, BLOCK, part), bf16)
    few = pltpu.VMEM((slots, BLOCK, part), bf16)
    table = pltpu.VMEM((2 * BLOCK, groups * 2 * BLOCK), bf16)
    column = pltpu.VMEM((blocks, BLOCK, HD), bf16)
    sums = pltpu.VMEM((blocks, BLOCK, HD), jnp.float32)
    dma = pltpu.SemaphoreType.DMA
    like = jax.ShapeDtypeStruct((2, BLOCK, width), bf16)
    return pl.pallas_call(
        functools.partial(fused_kernel, n, heads, slots),
        out_shape=[like] * 4,
        in_specs=[SMEM_SPEC, VMEM_SPEC] + [ANY_SPEC] * 8,
        out_specs=[ANY_SPEC] * 4,
        scratch_shapes=[local] * 10
        + [mine] * 2
        + [few] * 4
        + [pltpu.VMEM((2, groups, 2 * BLOCK), jnp.float32)]
        + [table] * 2
        + [mine] * 2
        + [local] * 2
        + [pltpu.VMEM((3, rows, width), bf16), pltpu.VMEM((2,) + weight.shape[1:], bf16)]
        + [
            pltpu.VMEM((2 * chips, tiles, rows, tile), jnp.float32),
            pltpu.VMEM((chips, tiles, rows, tile), jnp.float32),
            pltpu.VMEM((chips - 1, tiles, rows, tile), bf16),
            pltpu.VMEM((chips - 1, tiles, rows, tile), bf16),
        ]
        + [column] * 4
        + [
            pltpu.VMEM((blocks * BLOCK, HD), bf16),
            pltpu.VMEM((HD, blocks * BLOCK), bf16),
            pltpu.VMEM((blocks * BLOCK, HD), bf16),
            pltpu.VMEM((stored, tile, tile), jnp.float32),
            pltpu.VMEM((blocks // 2, 1, tile), jnp.float32),
        ]
        + [sums] * 3
        + [column] * 3
        + [pltpu.SMEM((blocks,), jnp.int32)] * 7
        + [pltpu.SMEM((slots,), jnp.int32)] * 2
        + [
            dma((8,)), dma((3,)), dma((heads,)), dma((7,)), dma((7, n)), dma((7, n)),
            dma((4, n // 2)), dma((4, n // 2)), dma((4,)), dma((2,)), dma((2,)),
            dma((2, chips, tiles)), dma((2, chips, tiles)),
        ],
        compiler_params=pltpu.CompilerParams(
            collective_id=collective, has_side_effects=True, vmem_limit_bytes=63 * 2**20
        ),
    )(order, filters, *[t.reshape(2, BLOCK, width) for t in tensors[:-1]], weight)


def land_kernel(count, *refs):
    sources, targets, held = refs[:count], refs[count : 2 * count], refs[2 * count : 3 * count]
    take, put = refs[3 * count :]
    arrive = [pltpu.make_async_copy(sources[i], held[i], take.at[i]) for i in range(count)]
    leave = [pltpu.make_async_copy(held[i], targets[i], put.at[i]) for i in range(count)]
    for copy in arrive:
        copy.start()
    for i in range(count):
        arrive[i].wait()
        leave[i].start()
    for copy in leave:
        copy.wait()


def land(*arrays):
    count = len(arrays)
    return pl.pallas_call(
        functools.partial(land_kernel, count),
        out_shape=[jax.ShapeDtypeStruct(a.shape, a.dtype) for a in arrays],
        in_specs=[ANY_SPEC] * count,
        out_specs=[ANY_SPEC] * count,
        scratch_shapes=[pltpu.VMEM(a.shape, a.dtype) for a in arrays]
        + [pltpu.SemaphoreType.DMA((count,))] * 2,
    )(*arrays)


def column_device(
    block_order, queries, keys, values, hyena_q, hyena_k, hyena_v, hyena_grad, filters, proj_weight
):
    n = lax.axis_size("seq")
    heads = lax.axis_size("head")
    held = block_order.shape[0] // 2
    few = held // 2 + 1
    follows = block_order[None, :] == block_order[:, None] + 1
    ids = jnp.arange(2 * held, dtype=jnp.int32)
    first = ids < held
    leaving = jnp.sum(follows & first[:, None] & ~first[None, :], dtype=jnp.int32)
    coming = jnp.sum(follows & ~first[:, None] & first[None, :], dtype=jnp.int32)
    fits = jnp.maximum(leaving, coming) <= few

    def run(slots, collective):
        def call(*arrays):
            return tuple(land(*fused(n, heads, slots, collective, *arrays)))

        return call

    grads = lax.cond(
        fits, run(few, 0), run(held, 1), block_order, filters,
        hyena_q, hyena_k, hyena_v, hyena_grad, queries, keys, values, proj_weight,
    )
    return tuple(out.reshape(queries.shape) for out in grads)


def per_device(*arrays):
    queries, filters = arrays[1], arrays[8]
    n = lax.axis_size("seq")
    whole_heads = queries.shape[1] == n * HD and queries.shape[0] == 2 * BLOCK
    paired = lax.axis_size("head") % 2 == 0 and lax.axis_size("head") > 2
    split = n % 4 == 0 and filters.shape[0] % (8 * n) == 0
    if whole_heads and paired and split and KL == BLOCK == HD:
        return column_device(*arrays)
    return ring_device(*arrays)


def solution(mesh):
    placed = (
        P(),
        P("seq", "head"),
        P("seq", "head"),
        P("seq", "head"),
        P("seq", "head"),
        P("seq", "head"),
        P("seq", "head"),
        P("seq", "head"),
        P("head", None),
        P(None, None, "head"),
    )
    return jax.shard_map(
        per_device,
        mesh=mesh,
        in_specs=placed,
        out_specs=(P("seq", "head"), P("seq", "head"), P("seq", "head"), P("seq", "head")),
        check_vma=False,
    )
```

```python
import functools

import jax
import jax.numpy as jnp
from jax import lax
from jax.experimental import pallas as pl
from jax.experimental.pallas import tpu as pltpu
from jax.sharding import PartitionSpec as P

HD = 128
GROUP = 16
KL = 128
BLOCK = 128


def for_sending(x):

    def short(part):
        return part.astype(jnp.bfloat16) if part.dtype == jnp.float32 else part

    return jax.tree.map(short, x)


def passed_along(value, axis, steps):
    count = lax.axis_size(axis)
    pairs = [(source, (source + steps) % count) for source in range(count)]
    return lax.ppermute(value, axis, pairs)


def keep_state(current):
    return current


def ring_device(
    block_order, queries, keys, values, hyena_q, hyena_k, hyena_v, hyena_grad, filters, proj_weight
):
    seq_count = lax.axis_size("seq")
    my_index = lax.axis_index("seq")
    row_count = queries.shape[0]
    feature_width = queries.shape[1]
    head_count = feature_width // HD
    block_total = block_order.shape[0]
    offsets = jnp.arange(BLOCK, dtype=jnp.int32)
    block_ids = jnp.arange(block_total, dtype=jnp.int32)

    def block_positions(source):
        block_pair = lax.dynamic_slice_in_dim(block_order, 2 * source, 2)
        return jnp.concatenate([block_pair[0] * BLOCK + offsets, block_pair[1] * BLOCK + offsets])

    def holder_of(target):
        return jnp.sum(jnp.where(block_order == target, block_ids, 0))

    my_positions = block_positions(my_index)
    product_kv = (hyena_k.astype(jnp.float32) * hyena_v.astype(jnp.float32)).astype(jnp.bfloat16)
    product_dq = (hyena_grad.astype(jnp.float32) * hyena_q.astype(jnp.float32)).astype(jnp.bfloat16)
    my_blocks = [
        lax.dynamic_index_in_dim(block_order, 2 * my_index + portion, 0, keepdims=False)
        for portion in range(2)
    ]
    gathered_z, gathered_dc = (
        lax.all_gather(product_kv, "seq", axis=0, tiled=True),
        lax.all_gather(product_dq, "seq", axis=0, tiled=True),
    )
    group_count = filters.shape[0]
    channels = hyena_q.shape[1]
    out_rows = jnp.arange(BLOCK)[:, None, None]
    window_rows = jnp.arange(BLOCK + KL)[None, :, None]
    tap_ids = jnp.arange(KL)[None, None, :]
    causal_table = (out_rows + KL - window_rows == tap_ids).astype(jnp.float32)
    anti_table = (window_rows - out_rows == tap_ids).astype(jnp.float32)
    causal_toeplitz = jnp.einsum(
        "gj,tsj->gts", filters, causal_table, precision=lax.Precision.HIGHEST
    )
    anti_toeplitz = jnp.einsum("gj,tsj->gts", filters, anti_table, precision=lax.Precision.HIGHEST)

    def apply_groups(toeplitz, window):
        grouped = window.astype(jnp.float32).reshape(BLOCK + KL, group_count, GROUP)
        result = jnp.einsum("gts,sgk->tgk", toeplitz, grouped, precision=lax.Precision.HIGHEST)
        return result.reshape(BLOCK, channels)

    conv_parts = []
    back_parts = []
    for portion in range(2):
        block_id = my_blocks[portion]
        before = lax.dynamic_slice_in_dim(
            gathered_z, holder_of(block_id - 1) * BLOCK + BLOCK - KL, KL, 0
        )
        before = jnp.where(block_id >= 1, before, jnp.zeros_like(before))
        after = lax.dynamic_slice_in_dim(gathered_dc, holder_of(block_id + 1) * BLOCK, KL, 0)
        after = jnp.where(block_id + 1 < block_total, after, jnp.zeros_like(after))
        own_z = product_kv[portion * BLOCK : (portion + 1) * BLOCK]
        own_dc = product_dq[portion * BLOCK : (portion + 1) * BLOCK]
        conv_parts.append(apply_groups(causal_toeplitz, jnp.concatenate([before, own_z])))
        back_parts.append(apply_groups(anti_toeplitz, jnp.concatenate([own_dc, after])))
    convolved = jnp.concatenate(conv_parts)
    back_conv = jnp.concatenate(back_parts)
    stacked = jnp.stack(
        [
            hyena_grad.astype(jnp.float32) * convolved,
            back_conv * hyena_v.astype(jnp.float32),
            back_conv * hyena_k.astype(jnp.float32),
        ]
    ).astype(jnp.bfloat16)
    summed = lax.psum_scatter(
        jnp.einsum("mic,mtc->it", proj_weight, stacked, preferred_element_type=jnp.float32),
        "head",
        scatter_dimension=0,
        tiled=True,
    )
    input_grad = summed.T.astype(jnp.bfloat16)
    score_scale = HD ** (-0.5)
    query_heads = queries.reshape(row_count, head_count, HD)
    key_heads = keys.reshape(row_count, head_count, HD)
    value_heads = values.reshape(row_count, head_count, HD)
    grad_heads = input_grad.reshape(row_count, head_count, HD)

    def tile_scores(query_block, key_block, query_pos, key_pos):
        scores = (
            jnp.einsum("qhd,khd->hqk", query_block, key_block, preferred_element_type=jnp.float32)
            * score_scale
        )
        allowed = (key_pos[None, :] <= query_pos[:, None])[None]
        return (scores, allowed)

    def stat_update(running, key_block, value_block, source):
        key_pos = block_positions(source)
        active = jnp.min(key_pos) <= jnp.max(my_positions)

        def stat_accumulate(current):
            row_max, row_sum, row_dot = current
            scores, allowed = tile_scores(query_heads, key_block, my_positions, key_pos)
            masked = jnp.where(allowed, scores, -1e30)
            new_max = jnp.maximum(row_max, jnp.max(masked, axis=2))
            terms = jnp.where(allowed, jnp.exp(masked - new_max[:, :, None]), 0.0)
            prob_grad = jnp.einsum(
                "qhd,khd->hqk", grad_heads, value_block, preferred_element_type=jnp.float32
            )
            factor = jnp.exp(row_max - new_max)
            return (
                new_max,
                row_sum * factor + jnp.sum(terms, axis=2),
                row_dot * factor + jnp.sum(terms * prob_grad, axis=2),
            )

        return lax.cond(active, stat_accumulate, keep_state, running)

    initial = (
        jnp.full((head_count, row_count), -1e30, jnp.float32),
        jnp.zeros((head_count, row_count), jnp.float32),
        jnp.zeros((head_count, row_count), jnp.float32),
    )

    def tile_grads(
        query_block, grad_block, norm_block, delta_block, query_pos, key_block, value_block, key_pos
    ):
        scores, allowed = tile_scores(query_block, key_block, query_pos, key_pos)
        probabilities = jnp.where(allowed, jnp.exp(scores - norm_block[:, :, None]), 0.0)
        prob_grad = jnp.einsum(
            "qhd,khd->hqk", grad_block, value_block, preferred_element_type=jnp.float32
        )
        score_grad = probabilities * (prob_grad - delta_block[:, :, None])
        probs_low = probabilities.astype(jnp.bfloat16)
        score_low = score_grad.astype(jnp.bfloat16)
        add_query = (
            jnp.einsum("hqk,khd->qhd", score_low, key_block, preferred_element_type=jnp.float32)
            * score_scale
        )
        add_key = (
            jnp.einsum("hqk,qhd->khd", score_low, query_block, preferred_element_type=jnp.float32)
            * score_scale
        )
        add_value = jnp.einsum(
            "hqk,qhd->khd", probs_low, grad_block, preferred_element_type=jnp.float32
        )
        return (add_query, add_key, add_value)

    zero_rows = jnp.zeros((row_count, head_count, HD), jnp.float32)

    def move_stat_queries(pair):
        return jax.tree.map(
            lambda part, own: part.astype(own.dtype),
            passed_along(for_sending(pair), "seq", 1),
            pair,
        )

    def stat_turn(turn_index, loop_state):
        running, key_block, value_block = loop_state
        source = (my_index - turn_index) % seq_count
        running = stat_update(running, key_block, value_block, source)
        key_block, value_block = move_stat_queries((key_block, value_block))
        return (running, key_block, value_block)

    loop_state = lax.fori_loop(0, seq_count - 1, stat_turn, (initial, key_heads, value_heads))
    running = stat_update(
        loop_state[0], loop_state[1], loop_state[2], (my_index - (seq_count - 1)) % seq_count
    )
    log_norm = running[0] + jnp.log(running[1])
    row_delta = running[2] / running[1]

    def query_turn(turn_index, loop_state):
        query_block, grad_block, norm_block, delta_block, query_acc, key_acc, value_acc = loop_state
        source = (my_index - turn_index) % seq_count
        query_pos = block_positions(source)
        active = jnp.min(my_positions) <= jnp.max(query_pos)

        def query_accumulate(current):
            add_query, add_key, add_value = tile_grads(
                query_block,
                grad_block,
                norm_block,
                delta_block,
                query_pos,
                key_heads,
                value_heads,
                my_positions,
            )
            return (current[0] + add_query, current[1] + add_key, current[2] + add_value)

        query_acc, key_acc, value_acc = lax.cond(
            active, query_accumulate, keep_state, (query_acc, key_acc, value_acc)
        )
        query_block, grad_block = passed_along((query_block, grad_block), "seq", 1)
        norm_block, delta_block, query_acc = passed_along(
            (norm_block, delta_block, query_acc), "seq", 1
        )
        return (query_block, grad_block, norm_block, delta_block, query_acc, key_acc, value_acc)

    final_state = lax.fori_loop(
        0,
        seq_count,
        query_turn,
        (query_heads, grad_heads, log_norm, row_delta, zero_rows, zero_rows, zero_rows),
    )
    query_total = final_state[4]
    key_total = final_state[5]
    value_total = final_state[6]
    query_grad = query_total.reshape(row_count, feature_width).astype(jnp.bfloat16)
    key_grad = key_total.reshape(row_count, feature_width).astype(jnp.bfloat16)
    value_grad = value_total.reshape(row_count, feature_width).astype(jnp.bfloat16)
    return (input_grad, query_grad, key_grad, value_grad)


MESH = pl.DeviceIdType.MESH
VMEM_SPEC = pl.BlockSpec(memory_space=pltpu.VMEM)
ANY_SPEC = pl.BlockSpec(memory_space=pl.ANY)
SMEM_SPEC = pl.BlockSpec(memory_space=pltpu.SMEM)


LOG2E = 1.4426950408889634


def aligned(index, size):
    return pl.ds(pl.multiple_of(index * size, size), size)


def fused_kernel(
    n, heads, slots,
    order_ref, filters_ref, hq_in, hk_in, hv_in, hg_in, q_in, k_in, v_in, weight_in,
    grad_out, dq_ref, dk_ref, dv_ref,
    hq, hk, hv, hg, qs, ks, vs, z_own, dc_own, grad_ref,
    zc, dcc, z_out, dc_out, z_far, dc_far,
    lines, causal, anti, convc, dzc, conv, dz, stacked, weights,
    total, pair_in, line_out, line_in,
    qc, kc, vc, gc, keys, keys_t, values, prob, inverse, dq_sum, dk_sum, dv_sum, dq_low, dk_low, dv_low,
    holder, after, before, z_cross, dc_cross, z_rank, dc_rank, z_pick, dc_pick,
    load_sem, weight_sem, last_sem, own_sem, send_sem, recv_sem,
    half_send, half_recv, half_own, far_send, far_recv, pair_sem, line_sem,
):
    me = lax.axis_index("seq")
    head = lax.axis_index("head")
    chips = heads // 2
    chip, core = head // 2, lax.rem(head, 2)
    partner = chip * 2 + 1 - core
    along = [lax.rem(chip + step, chips) for step in range(chips)]
    steps = list(range(1, chips)) + [0]
    blocks = order_ref.shape[0]
    members = n // 2
    held = blocks // 2
    side, place = me // members, lax.rem(me, members)
    base = side * held
    width = hq.shape[2]
    part = zc.shape[2]
    groups = part // GROUP
    tile = 2 * BLOCK
    tiles = width // tile

    loads = [
        pltpu.make_async_copy(source, target, load_sem.at[i])
        for i, (source, target) in enumerate(
            ((hg_in, hg), (hq_in, hq), (hk_in, hk), (hv_in, hv), (q_in, qs), (k_in, ks), (v_in, vs))
        )
    ]
    for copy in loads:
        copy.start()

    def weight_copy(m, slot):
        return pltpu.make_async_copy(weight_in.at[m], weights.at[slot], weight_sem.at[m])

    barrier = pltpu.get_barrier_semaphore()
    for step in range(1, n):
        pl.semaphore_signal(
            barrier, inc=1, device_id={"seq": lax.rem(me + step, n)}, device_id_type=MESH
        )
    head_peers = [partner] + [along[step] * 2 + core for step in range(1, chips)]
    for peer in head_peers:
        pl.semaphore_signal(barrier, inc=1, device_id={"head": peer}, device_id_type=MESH)

    def wide_of(ref):
        return ref[...].astype(jnp.float32)

    loads[0].wait()
    loads[1].wait()
    dc_own[...] = (wide_of(hg) * wide_of(hq)).astype(jnp.bfloat16)
    loads[2].wait()
    loads[3].wait()
    z_own[...] = (wide_of(hk) * wide_of(hv)).astype(jnp.bfloat16)
    weight_copy(1, 0).start()
    weight_copy(2, 1).start()
    pl.semaphore_wait(barrier, n - 1 + len(head_peers))

    far_steps, near_steps = list(range(members)), list(range(members + 1, n))
    mixed = [s for both in zip(far_steps, near_steps) for s in both] + far_steps[len(near_steps) :]

    def peer_at(step):
        if step < members:
            return (1 - side) * members + lax.rem(place + step, members)
        return side * members + lax.rem(place + step - members, members)

    def to_head(tensor, src, dst, step):
        peer = peer_at(step)
        return pltpu.make_async_remote_copy(
            src_ref=src.at[:, :, aligned(peer, HD)], dst_ref=dst.at[aligned(me, 2)],
            send_sem=send_sem.at[tensor, step], recv_sem=recv_sem.at[tensor, step],
            device_id={"seq": peer}, device_id_type=MESH,
        )

    def to_rows(tensor, src, dst, step):
        peer = peer_at(step)
        return pltpu.make_async_remote_copy(
            src_ref=src.at[aligned(peer, 2)], dst_ref=dst.at[:, :, aligned(me, HD)],
            send_sem=send_sem.at[tensor, step], recv_sem=recv_sem.at[tensor, step],
            device_id={"seq": peer}, device_id_type=MESH,
        )

    def own_head(tensor, src, dst):
        return pltpu.make_async_copy(
            src.at[:, :, aligned(me, HD)], dst.at[aligned(me, 2)], own_sem.at[tensor]
        )

    def own_rows(tensor, src, dst):
        return pltpu.make_async_copy(
            src.at[aligned(me, 2)], dst.at[:, :, aligned(me, HD)], own_sem.at[tensor]
        )

    def start_all(make, own, tensor, src, dst):
        for step in mixed:
            make(tensor, src, dst, step).start()
        own(tensor, src, dst).start()

    def wait_all(make, own, tensor, src, dst):
        for step in mixed:
            make(tensor, src, dst, step).wait()
        own(tensor, src, dst).wait()

    def spread(tensor, src, dst, step):
        goal = lax.rem(place + step, members)
        return pltpu.make_async_remote_copy(
            src_ref=src.at[:, :, aligned(goal, part)], dst_ref=dst.at[aligned(place, 2)],
            send_sem=half_send.at[tensor, step], recv_sem=half_recv.at[tensor, step],
            device_id={"seq": side * members + goal}, device_id_type=MESH,
        )

    def spread_own(tensor, src, dst):
        return pltpu.make_async_copy(
            src.at[:, :, aligned(place, part)], dst.at[aligned(place, 2)], half_own.at[tensor]
        )

    def collect(tensor, src, dst, step):
        goal = lax.rem(place + step, members)
        return pltpu.make_async_remote_copy(
            src_ref=src.at[aligned(goal, 2)], dst_ref=dst.at[:, :, aligned(place, part)],
            send_sem=half_send.at[tensor, step], recv_sem=half_recv.at[tensor, step],
            device_id={"seq": side * members + goal}, device_id_type=MESH,
        )

    def collect_own(tensor, src, dst):
        return pltpu.make_async_copy(
            src.at[aligned(place, 2)], dst.at[:, :, aligned(place, part)], half_own.at[tensor]
        )

    def cross(tensor, src, dst):
        return pltpu.make_async_remote_copy(
            src_ref=src, dst_ref=dst.at[pl.ds(0, slots)],
            send_sem=far_send.at[tensor], recv_sem=far_recv.at[tensor],
            device_id={"seq": lax.rem(me + members, n)}, device_id_type=MESH,
        )

    for tensor, src, dst in ((0, dc_own, dcc), (1, z_own, zc)):
        for step in range(1, members):
            spread(tensor, src, dst, step).start()
        spread_own(tensor, src, dst).start()
    loads[4].wait()
    loads[5].wait()
    inner = place // (members // 2) != side

    @pl.when(inner)
    def _():
        for step in far_steps:
            to_head(0, qs, qc, step).start()

    @pl.when(jnp.logical_not(inner))
    def _():
        for step in near_steps:
            to_head(0, qs, qc, step).start()

    order = [order_ref[r] for r in range(blocks)]
    for p in range(blocks):
        found = jnp.int32(0)
        for r in range(1, blocks):
            found = jnp.where(order[r] == p, r, found)
        holder[p] = found
    for start in (0, held):
        z_count, dc_count = jnp.int32(0), jnp.int32(0)
        for r in range(start, start + held):
            later = holder[jnp.minimum(order[r] + 1, blocks - 1)]
            later = jnp.where(order[r] + 1 < blocks, later, r)
            sooner = holder[jnp.maximum(order[r] - 1, 0)]
            sooner = jnp.where(order[r] > 0, sooner, r)
            leaves = (later < held) if start else (later >= held)
            returns = (sooner < held) if start else (sooner >= held)
            leaves = jnp.where(leaves, 1, 0)
            returns = jnp.where(returns, 1, 0)
            after[r], before[r] = later, sooner
            z_cross[r], dc_cross[r] = leaves, returns
            z_rank[r], dc_rank[r] = z_count, dc_count
            z_count, dc_count = z_count + leaves, dc_count + returns
    for pick, crossing, rank in ((dc_pick, dc_cross, dc_rank), (z_pick, z_cross, z_rank)):
        flags = [crossing[base + l] for l in range(held)]
        ranks = [rank[base + l] for l in range(held)]
        for k in range(slots):
            found = jnp.int32(0)
            for l in range(1, held):
                found = jnp.where((flags[l] == 1) & (ranks[l] == k), l, found)
            pick[k] = found

    for tensor, src, dst, pick, out, far in (
        (0, dc_own, dcc, dc_pick, dc_out, dc_far), (1, z_own, zc, z_pick, z_out, z_far)
    ):
        for step in range(1, members):
            spread(tensor, src, dst, step).wait()
        spread_own(tensor, src, dst).wait()
        for k in range(slots):
            out[k] = dst[pick[k]]
        cross(tensor, out, far).start()
    window = 2 * BLOCK
    taps = filters_ref[aligned(place, groups), :]
    flip = jnp.where(
        lax.broadcasted_iota(jnp.int32, (KL, KL), 0) + lax.broadcasted_iota(jnp.int32, (KL, KL), 1)
        == KL - 1, 1.0, 0.0,
    ).astype(jnp.bfloat16)
    high = taps.astype(jnp.bfloat16)
    low = (taps - high.astype(jnp.float32)).astype(jnp.bfloat16)
    turned = jnp.dot(high, flip, preferred_element_type=jnp.float32)
    turned = turned + jnp.dot(low, flip, preferred_element_type=jnp.float32)
    for at, rows in ((0, taps), (1, turned)):
        lines[at] = jnp.concatenate([rows, jnp.zeros_like(rows)], axis=1)

    def build(g, carry):
        lanes = aligned(g, window)
        for at, table in ((0, anti), (1, causal)):
            line = jnp.broadcast_to(lines[at, pl.ds(g, 1), :], (BLOCK, window))
            line = pltpu.roll(line, at, 1, stride=1, stride_axis=0)
            top = line.astype(jnp.bfloat16)
            table[:BLOCK, lanes] = top
            table[BLOCK:, lanes] = (line - top.astype(jnp.float32)).astype(jnp.bfloat16)
        return carry

    lax.fori_loop(0, groups, build, 0)

    lane_group = lax.broadcasted_iota(jnp.int32, (window, window), 1) % HD // GROUP
    chunks = part // HD
    chunk_groups = groups // chunks

    def filtered(goal, near, far, linked, end, rank, table, target, own_first):
        pairs = []
        for half in range(2):
            local = goal * 2 + half
            row = base + local
            own = near[local]
            link = linked[row]
            inside = (link >= base) & (link < base + held)
            some = jnp.where(order_ref[row] == end, 0.0, 1.0)
            here = jnp.where(inside, some, 0.0)
            there = jnp.where(inside, 0.0, some)
            found = near[jnp.where(inside, link - base, 0)].astype(jnp.float32) * here
            sent = far[jnp.where(inside, 0, jnp.minimum(rank[link], slots - 1))]
            other = (found + sent.astype(jnp.float32) * there).astype(jnp.bfloat16)
            pairs.append((own, other) if own_first else (other, own))
        for c in range(chunks):
            lanes = slice(c * HD, (c + 1) * HD)
            wide = jnp.concatenate(
                [jnp.concatenate([a[:, lanes], b[:, lanes]], axis=0) for a, b in pairs], axis=1
            )
            stack = jnp.concatenate(
                [
                    jnp.where(lane_group == g, wide, jnp.zeros_like(wide))
                    for g in range(chunk_groups)
                ],
                axis=0,
            )
            span = chunk_groups * window
            result = jnp.dot(
                table[:, c * span : (c + 1) * span], stack, preferred_element_type=jnp.float32
            )
            result = (result[:BLOCK] + result[BLOCK:]).astype(target.dtype)
            target[goal * 2, :, lanes] = result[:, :HD]
            target[goal * 2 + 1, :, lanes] = result[:, HD:]

    def send_back(tensor, near, far, linked, end, rank, table, target, out, own_first):
        def one(step, carry):
            goal = lax.rem(place + step, members)
            filtered(goal, near, far, linked, end, rank, table, target, own_first)

            @pl.when(step < members)
            def _():
                collect(tensor, target, out, step).start()

            return carry

        lax.fori_loop(1, members + 1, one, 0)
        collect_own(tensor, target, out).start()

    def returned(tensor, target, out):
        for step in range(1, members):
            collect(tensor, target, out, step).wait()
        collect_own(tensor, target, out).wait()

    def rows_of(value):
        return value.reshape(tile, width)

    cross(0, dc_out, dc_far).wait()
    send_back(2, dcc, dc_far, after, blocks - 1, dc_rank, anti, dzc, dz, True)
    cross(1, z_out, z_far).wait()

    @pl.when(inner)
    def _():
        for step in far_steps:
            to_head(1, ks, kc, step).start()

    @pl.when(jnp.logical_not(inner))
    def _():
        for step in far_steps:
            to_head(0, qs, qc, step).start()

    send_back(3, zc, z_far, before, 0, z_rank, causal, convc, conv, False)
    attention = ((0, qs, qc), (1, ks, kc), (2, vs, vc))

    @pl.when(inner)
    def _():
        for step in near_steps:
            to_head(0, qs, qc, step).start()

    @pl.when(jnp.logical_not(inner))
    def _():
        for step in far_steps:
            to_head(1, ks, kc, step).start()

    own_head(0, qs, qc).start()
    for step in near_steps:
        to_head(1, ks, kc, step).start()
    own_head(1, ks, kc).start()
    loads[6].wait()
    start_all(to_head, own_head, *attention[2])

    goals = []
    for step in steps:
        goals.append(along[step] * 2 + 1 - core)
        goals.append(along[step] * 2 + core)

    def last_weight(slot):
        rows = aligned(goals[slot], width)
        return pltpu.make_async_copy(
            weight_in.at[0, rows], weights.at[0, rows], last_sem.at[slot]
        )

    def product(m, slot, goal, j):
        return lax.dot_general(
            stacked[m], weights[slot, aligned(goal * tiles + j, tile), :],
            (((1,), (1,)), ((), ())), preferred_element_type=jnp.float32,
        )

    returned(2, dzc, dz)
    wide = wide_of(dz)
    stacked[1] = rows_of((wide * wide_of(hv)).astype(jnp.bfloat16))
    stacked[2] = rows_of((wide * wide_of(hk)).astype(jnp.bfloat16))
    weight_copy(1, 0).wait()
    weight_copy(2, 1).wait()
    for slot, goal in enumerate(goals):
        def begin(j, carry, slot=slot, goal=goal):
            total[slot, j] = product(1, 0, goal, j) + product(2, 1, goal, j)
            return carry

        lax.fori_loop(0, tiles, begin, 0)
        last_weight(slot).start()
    returned(3, convc, conv)
    stacked[0] = rows_of((wide_of(hg) * wide_of(conv)).astype(jnp.bfloat16))

    def pair_copy(at, j):
        return pltpu.make_async_remote_copy(
            src_ref=total.at[2 * at, j], dst_ref=pair_in.at[at, j],
            send_sem=pair_sem.at[0, at, j], recv_sem=pair_sem.at[1, at, j],
            device_id={"head": partner}, device_id_type=MESH,
        )

    def line_copy(at, j):
        return pltpu.make_async_remote_copy(
            src_ref=line_out.at[at, j], dst_ref=line_in.at[at, j],
            send_sem=line_sem.at[0, at, j], recv_sem=line_sem.at[1, at, j],
            device_id={"head": along[steps[at]] * 2 + core}, device_id_type=MESH,
        )

    for at in range(chips):
        last_weight(2 * at).wait()

        def give_pair(j, carry, at=at):
            total[2 * at, j] += product(0, 0, goals[2 * at], j)
            pair_copy(at, j).start()
            return carry

        lax.fori_loop(0, tiles, give_pair, 0)
        last_weight(2 * at + 1).wait()

        def keep(j, carry, at=at):
            value = total[2 * at + 1, j] + product(0, 0, goals[2 * at + 1], j)
            if at < chips - 1:
                pair_copy(at, j).wait()
                line_out[at, j] = (value + pair_in[at, j]).astype(line_out.dtype)
                line_copy(at, j).start()
            else:
                total[2 * at + 1, j] = value
            return carry

        lax.fori_loop(0, tiles, keep, 0)
    last = chips - 1
    for j in range(tiles):
        pair_copy(last, j).wait()
        value = total[2 * last + 1, j] + pair_in[last, j]
        for at in range(last):
            line_copy(at, j).wait()
            value = value + line_in[at, j].astype(jnp.float32)
        grad_ref[:, :, j * tile : (j + 1) * tile] = value.astype(grad_ref.dtype).reshape(
            2, BLOCK, tile
        )
    start_all(to_head, own_head, 3, grad_ref, gc)
    grad_copy = pltpu.make_async_copy(grad_ref, grad_out, load_sem.at[7])
    grad_copy.start()

    scale = HD ** (-0.5)
    contract_last = (((1,), (1,)), ((), ()))
    wait_all(to_head, own_head, *attention[0])
    wait_all(to_head, own_head, *attention[1])
    for b in range(blocks):
        here = slice(b * BLOCK, (b + 1) * BLOCK)
        rows = kc[holder[b]]
        keys[here, :] = rows
        keys_t[:, here] = rows.T

    def pair(ref, i):
        return jnp.concatenate([ref[holder[2 * i]], ref[holder[2 * i + 1]]], axis=0)

    def add(sums, value, i):
        value = value.reshape(2 * i + 2, BLOCK, HD)
        if i == blocks // 2 - 1:
            sums[...] = value
        else:
            sums[: 2 * i + 2] += value

    def chance_of(i):
        first = i * (i + 1) // 2
        terms = prob[first : first + i + 1].reshape((i + 1) * tile, tile)
        return terms * inverse[i]

    def give(sums, factor, low):
        for s in range(blocks):
            rows = sums[order_ref[s]]
            rows = rows if factor is None else rows * factor
            low[s] = rows.astype(low.dtype)

    key_at = lax.broadcasted_iota(jnp.int32, (tile, tile), 0)
    query_at = lax.broadcasted_iota(jnp.int32, (tile, tile), 1)
    rate = scale * LOG2E

    def folded(value, op):
        value = value.reshape(tile // 8, 8, tile)
        return op(value, axis=0)

    def chances(i, carry):
        q = pair(qc, i)
        first = i * (i + 1) // 2

        def score(j, top):
            value = lax.dot_general(
                keys[aligned(j, tile), :], q, contract_last, preferred_element_type=jnp.float32
            )
            prob[first + j] = value
            return jnp.maximum(top, folded(value, jnp.max))

        top = lax.fori_loop(0, i, score, jnp.full((8, tile), -1e30, jnp.float32))
        value = lax.dot_general(
            keys[aligned(i, tile), :], q, contract_last, preferred_element_type=jnp.float32
        )
        value = jnp.where(key_at <= query_at, value, -1e30)
        prob[first + i] = value
        top = jnp.maximum(top, folded(value, jnp.max))
        top = jnp.max(top, axis=0, keepdims=True)

        def term(j, sums):
            value = jnp.exp2((prob[first + j] - top) * rate)
            prob[first + j] = value
            return sums + folded(value, jnp.sum)

        sums = lax.fori_loop(0, i + 1, term, jnp.zeros((8, tile), jnp.float32))
        inverse[i] = 1.0 / jnp.sum(sums, axis=0, keepdims=True)
        return carry

    lax.fori_loop(0, blocks // 2, chances, 0)

    wait_all(to_head, own_head, 3, grad_ref, gc)
    for i in reversed(range(blocks // 2)):
        chance = chance_of(i).astype(jnp.bfloat16)
        add(dv_sum, jnp.dot(chance, pair(gc, i), preferred_element_type=jnp.float32), i)
    give(dv_sum, None, dv_low)
    start_all(to_rows, own_rows, 4, dv_low, dv_ref)
    wait_all(to_head, own_head, *attention[2])
    for b in range(blocks):
        values[b * BLOCK : (b + 1) * BLOCK, :] = vc[holder[b]]
    for i in reversed(range(blocks // 2)):
        depth = (i + 1) * tile
        prob_grad = lax.dot_general(
            values[:depth, :], pair(gc, i), contract_last, preferred_element_type=jnp.float32
        )
        chance = chance_of(i)
        delta = jnp.sum(chance * prob_grad, axis=0, keepdims=True)
        score_grad = (chance * (prob_grad - delta)).astype(jnp.bfloat16)
        add(dk_sum, jnp.dot(score_grad, pair(qc, i), preferred_element_type=jnp.float32), i)
        query_t = jnp.dot(keys_t[:, :depth], score_grad, preferred_element_type=jnp.float32)
        dq_sum[2 * i : 2 * i + 2] = (query_t.T * scale).reshape(2, BLOCK, HD)
    give(dq_sum, None, dq_low)
    start_all(to_rows, own_rows, 5, dq_low, dq_ref)
    give(dk_sum, scale, dk_low)
    start_all(to_rows, own_rows, 6, dk_low, dk_ref)
    grad_copy.wait()
    wait_all(to_rows, own_rows, 4, dv_low, dv_ref)
    wait_all(to_rows, own_rows, 5, dq_low, dq_ref)
    wait_all(to_rows, own_rows, 6, dk_low, dk_ref)


def fused(n, heads, slots, collective, order, filters, *tensors):
    rows, width = tensors[0].shape
    weight = tensors[-1]
    blocks = order.shape[0]
    held = blocks // 2
    chips = heads // 2
    part = width // (n // 2)
    groups = part // GROUP
    tile = 2 * BLOCK
    tiles = width // tile
    stored = (blocks // 2) * (blocks // 2 + 1) // 2
    bf16 = jnp.bfloat16
    local = pltpu.VMEM((2, BLOCK, width), bf16)
    mine = pltpu.VMEM((held, BLOCK, part), bf16)
    few = pltpu.VMEM((slots, BLOCK, part), bf16)
    table = pltpu.VMEM((2 * BLOCK, groups * 2 * BLOCK), bf16)
    column = pltpu.VMEM((blocks, BLOCK, HD), bf16)
    sums = pltpu.VMEM((blocks, BLOCK, HD), jnp.float32)
    dma = pltpu.SemaphoreType.DMA
    like = jax.ShapeDtypeStruct((2, BLOCK, width), bf16)
    return pl.pallas_call(
        functools.partial(fused_kernel, n, heads, slots),
        out_shape=[like] * 4,
        in_specs=[SMEM_SPEC, VMEM_SPEC] + [ANY_SPEC] * 8,
        out_specs=[ANY_SPEC] * 4,
        scratch_shapes=[local] * 10
        + [mine] * 2
        + [few] * 4
        + [pltpu.VMEM((2, groups, 2 * BLOCK), jnp.float32)]
        + [table] * 2
        + [mine] * 2
        + [local] * 2
        + [pltpu.VMEM((3, rows, width), bf16), pltpu.VMEM((2,) + weight.shape[1:], bf16)]
        + [
            pltpu.VMEM((2 * chips, tiles, rows, tile), jnp.float32),
            pltpu.VMEM((chips, tiles, rows, tile), jnp.float32),
            pltpu.VMEM((chips - 1, tiles, rows, tile), bf16),
            pltpu.VMEM((chips - 1, tiles, rows, tile), bf16),
        ]
        + [column] * 4
        + [
            pltpu.VMEM((blocks * BLOCK, HD), bf16),
            pltpu.VMEM((HD, blocks * BLOCK), bf16),
            pltpu.VMEM((blocks * BLOCK, HD), bf16),
            pltpu.VMEM((stored, tile, tile), jnp.float32),
            pltpu.VMEM((blocks // 2, 1, tile), jnp.float32),
        ]
        + [sums] * 3
        + [column] * 3
        + [pltpu.SMEM((blocks,), jnp.int32)] * 7
        + [pltpu.SMEM((slots,), jnp.int32)] * 2
        + [
            dma((8,)), dma((3,)), dma((heads,)), dma((7,)), dma((7, n)), dma((7, n)),
            dma((4, n // 2)), dma((4, n // 2)), dma((4,)), dma((2,)), dma((2,)),
            dma((2, chips, tiles)), dma((2, chips, tiles)),
        ],
        compiler_params=pltpu.CompilerParams(
            collective_id=collective, has_side_effects=True, vmem_limit_bytes=63 * 2**20
        ),
    )(order, filters, *[t.reshape(2, BLOCK, width) for t in tensors[:-1]], weight)


def land_kernel(count, *refs):
    sources, targets, held = refs[:count], refs[count : 2 * count], refs[2 * count : 3 * count]
    take, put = refs[3 * count :]
    arrive = [pltpu.make_async_copy(sources[i], held[i], take.at[i]) for i in range(count)]
    leave = [pltpu.make_async_copy(held[i], targets[i], put.at[i]) for i in range(count)]
    for copy in arrive:
        copy.start()
    for i in range(count):
        arrive[i].wait()
        leave[i].start()
    for copy in leave:
        copy.wait()


def land(*arrays):
    count = len(arrays)
    return pl.pallas_call(
        functools.partial(land_kernel, count),
        out_shape=[jax.ShapeDtypeStruct(a.shape, a.dtype) for a in arrays],
        in_specs=[ANY_SPEC] * count,
        out_specs=[ANY_SPEC] * count,
        scratch_shapes=[pltpu.VMEM(a.shape, a.dtype) for a in arrays]
        + [pltpu.SemaphoreType.DMA((count,))] * 2,
    )(*arrays)


def column_device(
    block_order, queries, keys, values, hyena_q, hyena_k, hyena_v, hyena_grad, filters, proj_weight
):
    n = lax.axis_size("seq")
    heads = lax.axis_size("head")
    held = block_order.shape[0] // 2
    few = held // 2 + 1
    ids = jnp.arange(2 * held, dtype=jnp.int32)
    follows = block_order[None, :] == block_order[:, None] + 1
    parted = (ids[None, :] < held) != (ids[:, None] < held)
    fits = jnp.sum((follows & parted).astype(jnp.int32)) <= 2 * few

    def run(slots, collective):
        def call(*arrays):
            return tuple(land(*fused(n, heads, slots, collective, *arrays)))

        return call

    grads = lax.cond(
        fits, run(few, 0), run(held, 1), block_order, filters,
        hyena_q, hyena_k, hyena_v, hyena_grad, queries, keys, values, proj_weight,
    )
    return tuple(out.reshape(queries.shape) for out in grads)


def per_device(*arrays):
    queries, filters = arrays[1], arrays[8]
    n = lax.axis_size("seq")
    whole_heads = queries.shape[1] == n * HD and queries.shape[0] == 2 * BLOCK
    paired = lax.axis_size("head") % 2 == 0 and lax.axis_size("head") > 2
    split = n % 4 == 0 and filters.shape[0] % (8 * n) == 0
    if whole_heads and paired and split and KL == BLOCK == HD:
        return column_device(*arrays)
    return ring_device(*arrays)


def solution(mesh):
    placed = (
        P(),
        P("seq", "head"),
        P("seq", "head"),
        P("seq", "head"),
        P("seq", "head"),
        P("seq", "head"),
        P("seq", "head"),
        P("seq", "head"),
        P("head", None),
        P(None, None, "head"),
    )
    return jax.shard_map(
        per_device,
        mesh=mesh,
        in_specs=placed,
        out_specs=(P("seq", "head"), P("seq", "head"), P("seq", "head"), P("seq", "head")),
        check_vma=False,
    )
```
